512 devices in a mesh: dp: 32 (over z_lo, y, core), expert: 16 (over z_hi, x).
Axes of the slice: x: 4, y: 4, z: 16 (z_hi: 4, z_lo: 4; z = z_hi * 4 + z_lo), core: 2. Of those that a mesh axis runs over, the one named last changes fastest.
Arguments:
- grad_out: bfloat16 [65536, 7168], P(('dp', 'expert')), may hold values from -6 to 6
- gate_weights: float32 [65536, 8], P(('dp', 'expert')), may hold values from 0.05 to 1
- route_ids: int32 [65536, 8], P(('dp', 'expert')), may hold values from 0 to 255, all different within a row
- replica_pick: int32 [65536, 8], P(('dp', 'expert')), may hold values from 0 to 1
- placement: int32 [32], replicated, may hold values from 0 to 255, as said below
- hidden_act: bfloat16 [32, 16, 32, 4, 1024], P('dp', None, 'expert'), may hold values from -6 to 6
- down_proj: bfloat16 [32, 7168, 1024], P('expert', 'dp'), may hold values from -0.1875 to 0.1875
Outputs:
- grad_w: bfloat16 [32, 7168, 1024], P('expert', 'dp')
- grad_gate: float32 [65536, 8], P(('dp', 'expert'))
The draws below stay inside these ranges and needn't reach their ends.
Inputs may be any that keep to these rules, and one draw needn't show every extreme that they name: `placement`: the 32 entries name 24 distinct experts; instance e * 2 and instance (e + 8) * 2 hold the same expert for e < 8; every other held expert is held by exactly one instance. `route_ids`: the 8 ids of a token differ.
All inputs are finite; a program needn't handle non-finite values.
Results may differ from the reference program's by a relative error of at most 0.0056.
Values may be sent and summed in bfloat16 or wider, within the bound.
No kernel may reach another device: no remote copies, remote signals or barrier semaphores. Data moves between devices by JAX's collectives and lax.ppermute only.
A program may use at most 128 MiB of HBM per device.

```python
import math
import jax
import jax.numpy as jnp
import numpy as np
from jax import lax

D = 7168
TOP = 8
ALL_EXPERTS = 256
FF = 1024
EXP_DEV = 2
TOK_DEV = 128
INSTANCES = 32
EXPERTS = 24
CAP = 4
TOKENS = 65536
N_DP = 32
N_EXPERT = 16


def draw_placement(key, part):
    half_axis = N_EXPERT // 2
    middle_key = jax.random.fold_in(key, 11)
    order_key = jax.random.fold_in(key, 12)
    middle = (jax.random.permutation(middle_key, ALL_EXPERTS - 2).astype(jnp.int32) + 1)[:EXPERTS - 2]
    ends = jnp.array([0, ALL_EXPERTS - 1], dtype=jnp.int32)
    chosen = jnp.concatenate([ends, middle], axis=0)
    shuffled = chosen[jax.random.permutation(order_key, EXPERTS).astype(jnp.int32)]
    hot_experts = shuffled[:half_axis]
    cold_experts = shuffled[half_axis:].reshape(N_EXPERT, EXP_DEV - 1)
    first_slot = jnp.concatenate([hot_experts, hot_experts], axis=0)
    return jnp.concatenate([first_slot[:, None], cold_experts], axis=1).reshape(-1).astype(jnp.int32)


def touch_ends(result, key, low, high):
    spot = [jax.random.randint(jax.random.fold_in(key, axis), (), 0, length) for axis, length in enumerate(result.shape)]
    longest = result.shape.index(max(result.shape))
    next_to = spot[:longest] + [(spot[longest] + 1) % result.shape[longest]] + spot[longest + 1:]
    return result.at[tuple(spot)].set(low).at[tuple(next_to)].set(high)


def level_of(stream_key, extent, cuts, smallest, high):
    loudness = 1.0
    for dim, parts in cuts:
        draws = jax.random.uniform(jax.random.fold_in(jax.random.fold_in(stream_key, 6), dim), (parts,), jnp.float32, smallest / len(cuts), high / len(cuts))
        loudness = loudness * jnp.repeat(jnp.exp(draws), extent[dim] // parts).reshape((-1,) + (1,) * (len(extent) - 1 - dim))
    return loudness


def distinct(key, rows, count, top, lift):
    sequence = jax.random.permutation(jax.random.fold_in(key, 1), count)
    pull = sequence
    for power in range(3):
        pull = pull * pull // count
    pull = pull * lift // count
    chance = jax.random.randint(jax.random.fold_in(key, 2), (rows, count), 0, 4096) + pull
    sure = jax.random.permutation(jax.random.fold_in(key, 3), rows)[jnp.arange(count) % rows]
    chance = jnp.where(jnp.arange(rows)[:, None] == sure[None, :], 1 << 14, chance)
    merit = chance * count + jnp.arange(count)
    return lax.top_k(merit.astype(jnp.int32), top)[1].astype(jnp.int32)


def bell_draw(own_key, extent, scale, bound, cuts=(), held_as=jnp.bfloat16):
    factor_of = level_of(own_key, extent, cuts, -0.22, 0.18) if cuts else 1.0
    values = jax.random.normal(own_key, extent, jnp.float32) * scale * factor_of
    return jnp.minimum(jnp.maximum(values, -bound), bound).astype(held_as)


def setup_inputs(seed: int = 0) -> dict:
    seeds = jax.random.split(jax.random.key(seed), 8)
    return {
        "grad_out": bell_draw(seeds[0], (TOKENS, D), 1.0, 6.0, ((0, 512),)),
        "gate_weights": jnp.clip(jnp.exp(math.log(1.0) - 2.9957323 * jax.random.uniform(seeds[1], (TOKENS, TOP), jnp.float32) ** level_of(seeds[1], (TOKENS, TOP), ((0, 512),), -0.2, 0.2)), 0.05, 1.0),
        "route_ids": distinct(seeds[2], TOKENS, ALL_EXPERTS, TOP, 512),
        "replica_pick": touch_ends(jax.random.randint(seeds[3], (TOKENS, TOP), 0, 2), jax.random.fold_in(seeds[3], 1), 0, 1).astype(jnp.int32),
        "placement": draw_placement(jax.random.fold_in(seeds[7], 71), 0),
        "hidden_act": bell_draw(seeds[5], (N_DP, N_EXPERT, INSTANCES, CAP, FF), 1.0, 6.0, ((0, 32), (2, 16))),
        "down_proj": bell_draw(seeds[6], (INSTANCES, D, FF), FF ** -0.5, 0.1875, ((0, 16), (1, 32))),
    }


def route_slots(flat_ids, flat_pick, placement, capacity):
    instances = placement.shape[0]
    numbers = jnp.arange(instances, dtype=jnp.int32)
    matches = placement[None, :] == flat_ids[:, None]
    held = jnp.any(matches, axis=1)
    first_copy = jnp.min(jnp.where(matches, numbers[None, :], instances), axis=1)
    last_copy = jnp.max(jnp.where(matches, numbers[None, :], -1), axis=1)
    target = jnp.where(flat_pick == 0, first_copy, last_copy).astype(jnp.int32)
    onehot = (target[:, None] == numbers[None, :]).astype(jnp.int32)
    earlier = (jnp.cumsum(onehot, axis=0) - onehot).astype(jnp.int32)
    slot_rank = jnp.sum(earlier * onehot, axis=1).astype(jnp.int32)
    kept_route = jnp.logical_and(held, slot_rank < capacity)
    position = jnp.where(kept_route, target * capacity + slot_rank, instances * capacity).astype(jnp.int32)
    return position, kept_route


def reference(grad_out, gate_weights, route_ids, replica_pick, placement, hidden_act, down_proj):
    sources = N_DP * N_EXPERT
    per_source = TOK_DEV * TOP
    total_slots = INSTANCES * CAP
    flat_ids = route_ids.reshape(sources, per_source)
    flat_pick = replica_pick.reshape(sources, per_source)

    def source_slots(ids_row, pick_row):
        return route_slots(ids_row, pick_row, placement, CAP)

    position, kept_route = jax.vmap(source_slots)(flat_ids, flat_pick)
    source_ids = jnp.arange(sources, dtype=jnp.int32)
    token_index = source_ids[:, None] * TOK_DEV + (jnp.arange(per_source, dtype=jnp.int32) // TOP)[None, :]
    gate_low = lax.optimization_barrier(gate_weights.astype(jnp.bfloat16)).astype(jnp.float32).reshape(sources, per_source)
    row_index = jnp.broadcast_to(source_ids[:, None], position.shape)
    table = jnp.full((sources, total_slots), -1, jnp.int32).at[row_index, position].set(token_index.astype(jnp.int32), mode="drop")
    gate_table = jnp.zeros((sources, total_slots), jnp.float32).at[row_index, position].set(gate_low, mode="drop")
    table = table.reshape(N_DP, N_EXPERT, INSTANCES, CAP)
    gate_table = gate_table.reshape(N_DP, N_EXPERT, INSTANCES, CAP)

    def instance_terms(instance):
        tokens_in = lax.dynamic_index_in_dim(table, instance, 2, False).reshape(-1)
        occupied = tokens_in >= 0
        rows_dy = jnp.where(occupied[:, None], grad_out[jnp.maximum(tokens_in, 0)], jnp.zeros((), jnp.bfloat16))
        gates_in = lax.dynamic_index_in_dim(gate_table, instance, 2, False).reshape(-1)
        hidden_rows = lax.dynamic_index_in_dim(hidden_act, instance, 2, False).reshape(-1, FF)
        weight = lax.dynamic_index_in_dim(down_proj, instance, 0, False)
        scaled = (gates_in[:, None] * rows_dy.astype(jnp.float32)).astype(jnp.bfloat16)
        weight_grad = jnp.dot(scaled.T, hidden_rows, preferred_element_type=jnp.float32)
        outputs = jnp.dot(hidden_rows, weight.T, preferred_element_type=jnp.float32)
        gate_grad = jnp.sum(outputs * rows_dy.astype(jnp.float32), axis=1)
        return weight_grad, gate_grad

    half_axis = N_EXPERT // 2

    def hot_pair(pair):
        first_grad, first_gate = instance_terms(pair * EXP_DEV)
        second_grad, second_gate = instance_terms((pair + half_axis) * EXP_DEV)
        return (first_grad + second_grad).astype(jnp.bfloat16), first_gate, second_gate

    hot_w, hot_first, hot_second = lax.map(hot_pair, jnp.arange(half_axis, dtype=jnp.int32))
    cold_list = jnp.asarray(np.array([device * EXP_DEV + column for device in range(N_EXPERT) for column in range(1, EXP_DEV)], dtype=np.int32))

    def cold_one(instance):
        weight_grad, gate_grad = instance_terms(instance)
        return weight_grad.astype(jnp.bfloat16), gate_grad

    cold_w, cold_gate = lax.map(cold_one, cold_list)
    hot_all = jnp.concatenate([hot_w, hot_w], axis=0)[:, None]
    grad_w = jnp.concatenate([hot_all, cold_w.reshape(N_EXPERT, EXP_DEV - 1, D, FF)], axis=1).reshape(INSTANCES, D, FF)
    gate_hot = jnp.concatenate([hot_first, hot_second], axis=0)[:, None]
    gate_all = jnp.concatenate([gate_hot, cold_gate.reshape(N_EXPERT, EXP_DEV - 1, N_DP * N_EXPERT * CAP)], axis=1)
    gate_all = gate_all.reshape(INSTANCES, N_DP, N_EXPERT, CAP).transpose(1, 2, 0, 3).reshape(sources, total_slots)
    picked = jnp.take_along_axis(gate_all, jnp.minimum(position, total_slots - 1).astype(jnp.int32), axis=1)
    grad_gate = jnp.where(kept_route, picked, jnp.zeros((), jnp.float32)).reshape(TOKENS, TOP)
    return grad_w, grad_gate
```

```python
import functools
import jax
import jax.numpy as jnp
from jax import lax
from jax.experimental import pallas as pl
from jax.experimental.pallas import tpu as pltpu
from jax.sharding import PartitionSpec as P

F32 = jnp.float32
BF16 = jnp.bfloat16
INSTANCES = 32
CAP = 4
TOP = 8
TOK = 128
SLOTS = INSTANCES * CAP
PIECE = 224
WIDE = 256


def route_masks(ids_ref, pick_ref, place_ref):
    rows = lax.broadcasted_iota(jnp.int32, (INSTANCES, TOK), 0)
    place = jnp.zeros((INSTANCES, TOK), jnp.int32)
    for i in range(INSTANCES):
        place = jnp.where(rows == i, place_ref[i], place)
    single = rows % 2 == 1
    first = rows < INSTANCES // 2
    masks = []
    for k in range(TOP):
        low = jnp.broadcast_to(pick_ref[k : k + 1, :], (INSTANCES, TOK)) == 0
        serves = jnp.logical_or(single, low == first)
        same = jnp.broadcast_to(ids_ref[k : k + 1, :], (INSTANCES, TOK)) == place
        masks.append(jnp.where(jnp.logical_and(same, serves), 1.0, 0.0).astype(F32))
    taken = functools.reduce(jnp.add, masks)
    before = (
        lax.broadcasted_iota(jnp.int32, (TOK, TOK), 0)
        < lax.broadcasted_iota(jnp.int32, (TOK, TOK), 1)
    ).astype(F32)
    rank = jnp.dot(taken.astype(BF16), before.astype(BF16), preferred_element_type=F32)
    return masks, taken, rank


def gather_kernel(place_ref, ids_ref, pick_ref, gate_ref, grad_ref, out_ref, select_ref):
    @pl.when(pl.program_id(0) == 0)
    def _():
        masks, taken, rank = route_masks(ids_ref, pick_ref, place_ref)
        gates = jnp.zeros((INSTANCES, TOK), F32)
        for k in range(TOP):
            low = gate_ref[k : k + 1, :].astype(BF16).astype(F32)
            gates = gates + masks[k] * jnp.broadcast_to(low, (INSTANCES, TOK))
        spread = (
            lax.broadcasted_iota(jnp.int32, (SLOTS, INSTANCES), 0) // CAP
            == lax.broadcasted_iota(jnp.int32, (SLOTS, INSTANCES), 1)
        ).astype(F32).astype(BF16)
        slot_rank = jnp.dot(spread, rank.astype(BF16), preferred_element_type=F32)
        slot_gate = jnp.dot(spread, gates.astype(BF16), preferred_element_type=F32)
        own = (lax.broadcasted_iota(jnp.int32, (SLOTS, TOK), 0) % CAP).astype(F32)
        select_ref[...] = jnp.where(slot_rank == own, slot_gate, 0.0).astype(BF16)

    rows = jnp.dot(select_ref[...], grad_ref[...], preferred_element_type=F32)
    blank = jnp.zeros((SLOTS, WIDE - PIECE), F32)
    for j in range(4):
        part = jnp.concatenate([rows[:, j * PIECE : (j + 1) * PIECE], blank], axis=1)
        out_ref[j] = part.astype(BF16)


def gather_rows(placement, ids, pick, gates, grad_out):
    width = grad_out.shape[1]
    steps = width // (4 * PIECE)
    whole = pl.BlockSpec((TOP, TOK), lambda s: (0, 0))
    return pl.pallas_call(
        gather_kernel,
        grid=(steps,),
        in_specs=[
            pl.BlockSpec(memory_space=pltpu.SMEM),
            whole,
            whole,
            whole,
            pl.BlockSpec((TOK, 4 * PIECE), lambda s: (0, s)),
        ],
        out_specs=pl.BlockSpec((4, SLOTS, WIDE), lambda s: (s, 0, 0)),
        out_shape=jax.ShapeDtypeStruct((steps * 4, SLOTS, WIDE), BF16),
        scratch_shapes=[pltpu.VMEM((SLOTS, TOK), BF16)],
        cost_estimate=pl.CostEstimate(
            flops=2 * SLOTS * TOK * width, bytes_accessed=4 * TOK * width, transcendentals=0
        ),
        name="gather_rows",
    )(placement, ids, pick, gates, grad_out)


def expert_kernel(rows_ref, hidden_ref, weight_ref, hot_ref, send_ref, cold_ref, gate_ref, acc_ref):
    step = pl.program_id(0)
    groups = hidden_ref.shape[0]
    count = rows_ref.shape[0] // 2
    both = rows_ref[...].astype(F32).reshape(count // 8, 2, 8, WIDE)
    even, odd = both[:, 0], both[:, 1]
    upper = lax.broadcasted_iota(jnp.int32, even.shape, 1) < CAP
    split = (
        jnp.where(upper, even, pltpu.roll(odd, 4, 1)),
        jnp.where(upper, pltpu.roll(even, 4, 1), odd),
    )
    ones = jnp.ones((8, PIECE), F32)
    for i in range(2):
        rows = split[i].reshape(count, WIDE)[:, :PIECE]
        hidden = hidden_ref[:, i].reshape(count, hidden_ref.shape[3])
        grad = lax.dot_general(
            rows.astype(BF16), hidden, (((0,), (0,)), ((), ())), preferred_element_type=F32
        )

        @pl.when(step == 0)
        def _():
            acc_ref[i] = grad

        @pl.when(step != 0)
        def _():
            acc_ref[i] += grad

        result = lax.dot_general(
            hidden, weight_ref[i], (((1,), (1,)), ((), ())), preferred_element_type=F32
        )
        dots = lax.dot_general(
            ones,
            result * rows,
            (((1,), (1,)), ((), ())),
            precision=lax.Precision.HIGHEST,
            preferred_element_type=F32,
        )
        span = count // groups
        for g in range(groups):
            gate_ref[g, i : i + 1, :] = dots[0:1, g * span : (g + 1) * span]

    @pl.when(step == pl.num_programs(0) - 1)
    def _():
        hot_ref[...] = acc_ref[0]
        send_ref[...] = acc_ref[0].astype(BF16)
        cold_ref[...] = acc_ref[1].astype(BF16)


def expert_grads(rows, hidden, weight):
    dp, _, span, ff = hidden.shape
    groups = 4
    steps = dp // groups
    fixed = lambda s: (0, 0)
    return pl.pallas_call(
        expert_kernel,
        grid=(steps,),
        in_specs=[
            pl.BlockSpec((groups * span * 2, WIDE), lambda s: (s, 0)),
            pl.BlockSpec((groups, 2, span, ff), lambda s: (s, 0, 0, 0)),
            pl.BlockSpec((2, PIECE, ff), lambda s: (0, 0, 0)),
        ],
        out_specs=[
            pl.BlockSpec((PIECE, ff), fixed),
            pl.BlockSpec((PIECE, ff), fixed),
            pl.BlockSpec((PIECE, ff), fixed),
            pl.BlockSpec((groups, 2, span), lambda s: (s, 0, 0)),
        ],
        out_shape=[
            jax.ShapeDtypeStruct((PIECE, ff), F32),
            jax.ShapeDtypeStruct((PIECE, ff), BF16),
            jax.ShapeDtypeStruct((PIECE, ff), BF16),
            jax.ShapeDtypeStruct((dp, 2, span), F32),
        ],
        scratch_shapes=[pltpu.VMEM((2, PIECE, ff), F32)],
        cost_estimate=pl.CostEstimate(
            flops=8 * dp * span * PIECE * ff,
            bytes_accessed=2 * hidden.size + 2 * rows.size + 2 * weight.size,
            transcendentals=0,
        ),
        name="expert_grads",
    )(rows, hidden, weight)


def pick_kernel(place_ref, ids_ref, pick_ref, gate_ref, back_ref, out_ref):
    masks, taken, rank = route_masks(ids_ref, pick_ref, place_ref)
    value = jnp.zeros((INSTANCES, TOK), F32)
    for c in range(CAP):
        column = jnp.broadcast_to(back_ref[:, c : c + 1], (INSTANCES, TOK))
        value = jnp.where(rank == c, column, value)
    for k in range(TOP):
        total = jnp.sum(masks[k] * value, axis=0, keepdims=True)
        low = gate_ref[k : k + 1, :].astype(BF16).astype(F32)
        out_ref[k : k + 1, :] = total / low


def pick_gates(placement, ids, pick, gates, back):
    vmem = pl.BlockSpec(memory_space=pltpu.VMEM)
    return pl.pallas_call(
        pick_kernel,
        in_specs=[pl.BlockSpec(memory_space=pltpu.SMEM)] + [vmem] * 4,
        out_specs=vmem,
        out_shape=jax.ShapeDtypeStruct((TOP, TOK), F32),
        name="pick_gates",
    )(placement, ids, pick, gates, back)


def per_device(grad_out, gate_weights, route_ids, replica_pick, placement, hidden_act, down_proj):
    dp, expert = lax.axis_size("dp"), lax.axis_size("expert")
    ff = hidden_act.shape[4]
    local = hidden_act[0].transpose(1, 0, 2, 3).reshape(1, 2, expert * CAP, ff)
    hidden = lax.all_gather(local, "dp", axis=0, tiled=True)
    ids, pick, gates = route_ids.T, replica_pick.T, gate_weights.T
    sent = gather_rows(placement, ids, pick, gates, grad_out)
    rows = lax.all_to_all(
        sent.reshape(dp * expert, 2 * CAP, WIDE),
        ("dp", "expert"),
        split_axis=0,
        concat_axis=0,
        tiled=True,
    )
    hot, hot_sent, cold, partial = expert_grads(
        rows.reshape(dp * expert * 2 * CAP, WIDE), hidden, down_proj
    )
    half = expert // 2
    other = lax.ppermute(hot_sent, "expert", [(e, (e + half) % expert) for e in range(expert)])
    spread = lax.all_to_all(partial, "dp", split_axis=0, concat_axis=0, tiled=True)
    own = jnp.sum(spread, axis=0).reshape(2, expert, CAP).transpose(1, 0, 2)
    back = lax.all_to_all(own, "expert", split_axis=0, concat_axis=0, tiled=True)
    grad_gate = pick_gates(placement, ids, pick, gates, back.reshape(INSTANCES, CAP)).T
    grad_w = jnp.stack([(hot + other.astype(F32)).astype(BF16), cold], axis=0)
    return grad_w, grad_gate


def solution(mesh):
    return jax.shard_map(
        per_device,
        mesh=mesh,
        in_specs=(
            P(("dp", "expert"), None),
            P(("dp", "expert"), None),
            P(("dp", "expert"), None),
            P(("dp", "expert"), None),
            P(),
            P("dp", None, "expert", None, None),
            P("expert", "dp", None),
        ),
        out_specs=(P("expert", "dp", None), P(("dp", "expert"), None)),
        check_vma=False,
    )
```

```python
import functools
import jax
import jax.numpy as jnp
from jax import lax
from jax.experimental import pallas as pl
from jax.experimental.pallas import tpu as pltpu
from jax.sharding import PartitionSpec as P


F32 = jnp.float32
BF16 = jnp.bfloat16
INSTANCES = 32
CAP = 4
TOP = 8
TOK = 128
SLOTS = INSTANCES * CAP
PIECE = 224
WIDE = 256


def route_masks(ids_ref, pick_ref, place_ref):
    rows = lax.broadcasted_iota(jnp.int32, (INSTANCES, TOK), 0)
    place = jnp.zeros((INSTANCES, TOK), jnp.int32)
    for i in range(INSTANCES):
        place = jnp.where(rows == i, place_ref[i], place)
    single = rows % 2 == 1
    first = rows < INSTANCES // 2
    masks = []
    for k in range(TOP):
        low = jnp.broadcast_to(pick_ref[k : k + 1, :], (INSTANCES, TOK)) == 0
        serves = jnp.logical_or(single, low == first)
        same = jnp.broadcast_to(ids_ref[k : k + 1, :], (INSTANCES, TOK)) == place
        masks.append(jnp.where(jnp.logical_and(same, serves), 1.0, 0.0).astype(F32))
    taken = functools.reduce(jnp.add, masks)
    before = (
        lax.broadcasted_iota(jnp.int32, (TOK, TOK), 0)
        < lax.broadcasted_iota(jnp.int32, (TOK, TOK), 1)
    ).astype(F32)
    rank = jnp.dot(taken.astype(BF16), before.astype(BF16), preferred_element_type=F32)
    return masks, taken, rank


def gather_kernel(place_ref, ids_ref, pick_ref, gate_ref, grad_ref, out_ref, select_ref):
    @pl.when(pl.program_id(0) == 0)
    def _():
        masks, _, rank = route_masks(ids_ref, pick_ref, place_ref)
        gates = jnp.zeros((INSTANCES, TOK), F32)
        for k in range(TOP):
            low = gate_ref[k : k + 1, :].astype(BF16).astype(F32)
            gates = gates + masks[k] * jnp.broadcast_to(low, (INSTANCES, TOK))
        spread = (
            lax.broadcasted_iota(jnp.int32, (SLOTS, INSTANCES), 0) // CAP
            == lax.broadcasted_iota(jnp.int32, (SLOTS, INSTANCES), 1)
        ).astype(F32).astype(BF16)
        slot_rank = jnp.dot(spread, rank.astype(BF16), preferred_element_type=F32)
        slot_gate = jnp.dot(spread, gates.astype(BF16), preferred_element_type=F32)
        own = (lax.broadcasted_iota(jnp.int32, (SLOTS, TOK), 0) % CAP).astype(F32)
        select_ref[...] = jnp.where(slot_rank == own, slot_gate, 0.0).astype(BF16)

    rows = jnp.dot(select_ref[...], grad_ref[...], preferred_element_type=F32)
    blank = jnp.zeros((SLOTS, WIDE - PIECE), F32)
    for j in range(4):
        part = jnp.concatenate([rows[:, j * PIECE : (j + 1) * PIECE], blank], axis=1)
        out_ref[j] = part.astype(BF16)


def gather_rows(placement, ids, pick, gates, grad_out):
    width = grad_out.shape[1]
    steps = width // (4 * PIECE)
    whole = pl.BlockSpec((TOP, TOK), lambda s: (0, 0))
    return pl.pallas_call(
        gather_kernel,
        grid=(steps,),
        in_specs=[
            pl.BlockSpec(memory_space=pltpu.SMEM),
            whole,
            whole,
            whole,
            pl.BlockSpec((TOK, 4 * PIECE), lambda s: (0, s)),
        ],
        out_specs=pl.BlockSpec((4, SLOTS, WIDE), lambda s: (s, 0, 0)),
        out_shape=jax.ShapeDtypeStruct((steps * 4, SLOTS, WIDE), BF16),
        scratch_shapes=[pltpu.VMEM((SLOTS, TOK), BF16)],
        cost_estimate=pl.CostEstimate(
            flops=2 * SLOTS * TOK * width, bytes_accessed=4 * TOK * width, transcendentals=0
        ),
        name="gather_rows",
    )(placement, ids, pick, gates, grad_out)


def swap_halves(first, second):
    count, lanes = first.shape
    first, second = first.reshape(count // 8, 8, lanes), second.reshape(count // 8, 8, lanes)
    upper = lax.broadcasted_iota(jnp.int32, first.shape, 1) < CAP
    return (
        jnp.where(upper, first, pltpu.roll(second, 4, 1)).reshape(count, lanes),
        jnp.where(upper, pltpu.roll(first, 4, 1), second).reshape(count, lanes),
    )


def instance_rows(rows_ref):
    count = rows_ref.shape[0] // 2
    both = rows_ref[...].astype(F32).reshape(count // 8, 2, 8, WIDE)
    return swap_halves(both[:, 0].reshape(count, WIDE), both[:, 1].reshape(count, WIDE))


def gate_kernel(place_ref, rows_ref, hidden_ref, weight_ref, gate_ref):
    split = instance_rows(rows_ref)
    count = rows_ref.shape[0] // 2
    folded = []
    for i in range(2):
        hidden = hidden_ref[:, 0, i].reshape(count, hidden_ref.shape[4])
        result = lax.dot_general(
            hidden, weight_ref[i], (((1,), (1,)), ((), ())), preferred_element_type=F32
        )
        product = result * split[i][:, :PIECE]
        blank = jnp.zeros((count, WIDE - PIECE), F32)
        tail = jnp.concatenate([product[:, 128:PIECE], blank], axis=1)
        folded.append(product[:, :128] + tail)
    even, odd = swap_halves(*folded)
    both = jnp.concatenate(
        [even.reshape(count // 8, 1, 8, 128), odd.reshape(count // 8, 1, 8, 128)], axis=1
    )
    both = both.reshape(count * 2 // 128, 128, 128)
    for g in range(count * 2 // 128):
        gate_ref[g] = jnp.sum(both[g].T, axis=0, keepdims=True)


def gate_parts(place, rows, hidden, weight):
    lines, steps, _, span, ff = hidden.shape
    dp = lines * steps
    return pl.pallas_call(
        gate_kernel,
        grid_spec=pltpu.PrefetchScalarGridSpec(
            num_scalar_prefetch=1,
            grid=(steps,),
            in_specs=[
                pl.BlockSpec((lines * span * 2, WIDE), lambda s, m: (s, 0)),
                pl.BlockSpec(
                    (lines, 1, 2, span, ff),
                    lambda s, m: (0, lax.rem(m[0] - s + steps, steps), 0, 0, 0),
                ),
                pl.BlockSpec((2, PIECE, ff), lambda s, m: (0, 0, 0)),
            ],
            out_specs=pl.BlockSpec((lines, 1, 2 * span), lambda s, m: (s, 0, 0)),
        ),
        out_shape=jax.ShapeDtypeStruct((dp, 1, 2 * span), F32),
        cost_estimate=pl.CostEstimate(
            flops=4 * dp * span * PIECE * ff,
            bytes_accessed=2 * hidden.size + 2 * rows.size + 2 * weight.size,
            transcendentals=0,
        ),
        name="gate_parts",
    )(place, rows, hidden, weight)


def grad_kernel(place_ref, rows_ref, hidden_ref, hot_ref, send_ref, out_ref, acc_ref):
    step = pl.program_id(0)
    split = instance_rows(rows_ref)
    count = rows_ref.shape[0] // 2
    for i in range(2):
        hidden = hidden_ref[:, 0, i].reshape(count, hidden_ref.shape[4])
        grad = lax.dot_general(
            split[i][:, :PIECE].astype(BF16),
            hidden,
            (((0,), (0,)), ((), ())),
            preferred_element_type=F32,
        )

        @pl.when(step == 0)
        def _():
            acc_ref[i] = grad

        @pl.when(step != 0)
        def _():
            acc_ref[i] += grad

    @pl.when(step == pl.num_programs(0) - 1)
    def _():
        hot_ref[...] = acc_ref[0]
        send_ref[...] = acc_ref[0].astype(BF16)
        out_ref[0] = acc_ref[1].astype(BF16)


def weight_parts(place, rows, hidden):
    lines, steps, _, span, ff = hidden.shape
    dp = lines * steps
    fixed = lambda s, m: (0, 0)
    return pl.pallas_call(
        grad_kernel,
        grid_spec=pltpu.PrefetchScalarGridSpec(
            num_scalar_prefetch=1,
            grid=(steps,),
            in_specs=[
                pl.BlockSpec((lines * span * 2, WIDE), lambda s, m: (s, 0)),
                pl.BlockSpec(
                    (lines, 1, 2, span, ff),
                    lambda s, m: (0, lax.rem(m[0] - s + steps, steps), 0, 0, 0),
                ),
            ],
            out_specs=[
                pl.BlockSpec((PIECE, ff), fixed),
                pl.BlockSpec((PIECE, ff), fixed),
                pl.BlockSpec((1, PIECE, ff), lambda s, m: (1, 0, 0)),
            ],
            scratch_shapes=[pltpu.VMEM((2, PIECE, ff), F32)],
        ),
        out_shape=[
            jax.ShapeDtypeStruct((PIECE, ff), F32),
            jax.ShapeDtypeStruct((PIECE, ff), BF16),
            jax.ShapeDtypeStruct((2, PIECE, ff), BF16),
        ],
        cost_estimate=pl.CostEstimate(
            flops=4 * dp * span * PIECE * ff,
            bytes_accessed=2 * hidden.size + 2 * rows.size,
            transcendentals=0,
        ),
        name="weight_parts",
    )(place, rows, hidden)


def pair_kernel(hot_ref, other_ref, grad_ref, out_ref):
    out_ref[0] = (hot_ref[...] + other_ref[...].astype(F32)).astype(BF16)


def pair_sum(hot, other, grad):
    ff = hot.shape[1]
    whole = pl.BlockSpec((PIECE, ff), lambda s: (0, 0))
    return pl.pallas_call(
        pair_kernel,
        grid=(1,),
        in_specs=[whole, whole, pl.BlockSpec(memory_space=pl.ANY)],
        out_specs=pl.BlockSpec((1, PIECE, ff), lambda s: (0, 0, 0)),
        out_shape=jax.ShapeDtypeStruct(grad.shape, BF16),
        input_output_aliases={2: 0},
        name="pair_sum",
    )(hot, other, grad)


def total_kernel(parts_ref, out_ref):
    total = jnp.sum(parts_ref[...], axis=0)
    for e in range(out_ref.shape[0]):
        out_ref[e] = total[:, e * 2 * CAP : (e + 1) * 2 * CAP]


def gate_totals(parts, expert):
    vmem = pl.BlockSpec(memory_space=pltpu.VMEM)
    return pl.pallas_call(
        total_kernel,
        in_specs=[vmem],
        out_specs=vmem,
        out_shape=jax.ShapeDtypeStruct((expert, 1, 2 * CAP), F32),
        name="gate_totals",
    )(parts)


def pick_kernel(place_ref, ids_ref, pick_ref, gate_ref, back_ref, out_ref):
    masks, _, rank = route_masks(ids_ref, pick_ref, place_ref)
    experts = back_ref.shape[0]
    spread = (
        lax.broadcasted_iota(jnp.int32, (INSTANCES, experts), 0) // 2
        == lax.broadcasted_iota(jnp.int32, (INSTANCES, experts), 1)
    ).astype(F32)
    back = jnp.dot(
        spread,
        back_ref[...].reshape(experts, 2 * CAP),
        precision=lax.Precision.HIGHEST,
        preferred_element_type=F32,
    )
    odd = lax.broadcasted_iota(jnp.int32, (INSTANCES, 1), 0) % 2 == 1
    value = jnp.zeros((INSTANCES, TOK), F32)
    for c in range(CAP):
        column = jnp.where(odd, back[:, CAP + c : CAP + c + 1], back[:, c : c + 1])
        value = jnp.where(rank == c, jnp.broadcast_to(column, (INSTANCES, TOK)), value)
    for k in range(TOP):
        total = jnp.sum(masks[k] * value, axis=0, keepdims=True)
        low = gate_ref[k : k + 1, :].astype(BF16).astype(F32)
        out_ref[k : k + 1, :] = total / low


def pick_gates(placement, ids, pick, gates, back):
    vmem = pl.BlockSpec(memory_space=pltpu.VMEM)
    return pl.pallas_call(
        pick_kernel,
        in_specs=[pl.BlockSpec(memory_space=pltpu.SMEM)] + [vmem] * 4,
        out_specs=vmem,
        out_shape=jax.ShapeDtypeStruct((TOP, TOK), F32),
        name="pick_gates",
    )(placement, ids, pick, gates, back)


LINES = ("y", "c")
EXPERT = ("zh", "x")
GROUPS = ("zl",) + LINES
EVERY = GROUPS + EXPERT


def layer(grad_out, gate_weights, route_ids, replica_pick, placement, hidden_act, down_proj):
    dp, expert = lax.axis_size(GROUPS), lax.axis_size(EXPERT)
    depth = lax.axis_size("zl")
    ff = hidden_act.shape[4]
    local = hidden_act[0].transpose(1, 0, 2, 3).reshape(1, 1, 2, expert * CAP, ff)
    column = [local] + [
        lax.ppermute(local, "zl", [(z, (z + d) % depth) for z in range(depth)])
        for d in range(1, depth)
    ]
    column = jnp.concatenate(column, axis=1)
    hidden = lax.all_gather(column, LINES, axis=0, tiled=True)
    place = lax.axis_index("zl").astype(jnp.int32).reshape(1)
    ids, pick, gates = route_ids.T, replica_pick.T, gate_weights.T
    sent = gather_rows(placement, ids, pick, gates, grad_out)
    sent = sent.reshape(dp * expert, 2 * CAP, WIDE)
    rows = lax.all_to_all(sent, EVERY, split_axis=0, concat_axis=0, tiled=True)
    rows = rows.reshape(dp * expert * 2 * CAP, WIDE)
    parts = gate_parts(place, rows, hidden, down_proj)
    parts = lax.all_to_all(parts, GROUPS, split_axis=0, concat_axis=0, tiled=True)
    hot, hot_sent, grad = weight_parts(place, rows, hidden)
    half = expert // 2
    other = lax.ppermute(hot_sent, EXPERT, [(e, (e + half) % expert) for e in range(expert)])
    own = gate_totals(parts, expert)
    back = lax.all_to_all(own, EXPERT, split_axis=0, concat_axis=0, tiled=True)
    grad_gate = pick_gates(placement, ids, pick, gates, back).T
    return pair_sum(hot, other, grad), grad_gate


def solution(mesh):
    fine = jax.sharding.Mesh(mesh.devices.reshape(4, 4, 2, 4, 4), EVERY)
    token = P(EVERY, None)
    return jax.shard_map(
        layer,
        mesh=fine,
        in_specs=(
            token,
            token,
            token,
            token,
            P(),
            P(GROUPS, None, EXPERT, None, None),
            P(EXPERT, GROUPS, None),
        ),
        out_specs=(P(EXPERT, GROUPS, None), token),
        check_vma=False,
    )
```

```python
import functools
import jax
import jax.numpy as jnp
from jax import lax
from jax.experimental import pallas as pl
from jax.experimental.pallas import tpu as pltpu
from jax.sharding import PartitionSpec as P


F32 = jnp.float32
BF16 = jnp.bfloat16
INSTANCES = 32
CAP = 4
TOP = 8
TOK = 128
SLOTS = INSTANCES * CAP
PIECE = 224
WIDE = 256


def route_masks(ids_ref, pick_ref, place_ref):
    rows = lax.broadcasted_iota(jnp.int32, (INSTANCES, TOK), 0)
    place = jnp.zeros((INSTANCES, TOK), jnp.int32)
    for i in range(INSTANCES):
        place = jnp.where(rows == i, place_ref[i], place)
    single = rows % 2 == 1
    first = rows < INSTANCES // 2
    masks = []
    for k in range(TOP):
        low = jnp.broadcast_to(pick_ref[k : k + 1, :], (INSTANCES, TOK)) == 0
        serves = jnp.logical_or(single, low == first)
        same = jnp.broadcast_to(ids_ref[k : k + 1, :], (INSTANCES, TOK)) == place
        masks.append(jnp.where(jnp.logical_and(same, serves), 1.0, 0.0).astype(F32))
    taken = functools.reduce(jnp.add, masks)
    before = (
        lax.broadcasted_iota(jnp.int32, (TOK, TOK), 0)
        < lax.broadcasted_iota(jnp.int32, (TOK, TOK), 1)
    ).astype(F32)
    rank = jnp.dot(taken.astype(BF16), before.astype(BF16), preferred_element_type=F32)
    return masks, taken, rank


def gather_kernel(place_ref, ids_ref, pick_ref, gate_ref, grad_ref, out_ref, select_ref):
    @pl.when(pl.program_id(0) == 0)
    def _():
        masks, _, rank = route_masks(ids_ref, pick_ref, place_ref)
        gates = jnp.zeros((INSTANCES, TOK), F32)
        for k in range(TOP):
            low = gate_ref[k : k + 1, :].astype(BF16).astype(F32)
            gates = gates + masks[k] * jnp.broadcast_to(low, (INSTANCES, TOK))
        spread = (
            lax.broadcasted_iota(jnp.int32, (SLOTS, INSTANCES), 0) // CAP
            == lax.broadcasted_iota(jnp.int32, (SLOTS, INSTANCES), 1)
        ).astype(F32).astype(BF16)
        slot_rank = jnp.dot(spread, rank.astype(BF16), preferred_element_type=F32)
        slot_gate = jnp.dot(spread, gates.astype(BF16), preferred_element_type=F32)
        own = (lax.broadcasted_iota(jnp.int32, (SLOTS, TOK), 0) % CAP).astype(F32)
        select_ref[...] = jnp.where(slot_rank == own, slot_gate, 0.0).astype(BF16)

    rows = jnp.dot(select_ref[...], grad_ref[...], preferred_element_type=F32)
    blank = jnp.zeros((SLOTS, WIDE - PIECE), F32)
    for j in range(4):
        part = jnp.concatenate([rows[:, j * PIECE : (j + 1) * PIECE], blank], axis=1)
        out_ref[j] = part.astype(BF16)


def gather_rows(placement, ids, pick, gates, grad_out):
    width = grad_out.shape[1]
    steps = width // (4 * PIECE)
    whole = pl.BlockSpec((TOP, TOK), lambda s: (0, 0))
    return pl.pallas_call(
        gather_kernel,
        grid=(steps,),
        in_specs=[
            pl.BlockSpec(memory_space=pltpu.SMEM),
            whole,
            whole,
            whole,
            pl.BlockSpec((TOK, 4 * PIECE), lambda s: (0, s)),
        ],
        out_specs=pl.BlockSpec((4, SLOTS, WIDE), lambda s: (s, 0, 0)),
        out_shape=jax.ShapeDtypeStruct((steps * 4, SLOTS, WIDE), BF16),
        scratch_shapes=[pltpu.VMEM((SLOTS, TOK), BF16)],
        cost_estimate=pl.CostEstimate(
            flops=2 * SLOTS * TOK * width, bytes_accessed=4 * TOK * width, transcendentals=0
        ),
        name="gather_rows",
    )(placement, ids, pick, gates, grad_out)


def swap_halves(first, second):
    count, lanes = first.shape
    first, second = first.reshape(count // 8, 8, lanes), second.reshape(count // 8, 8, lanes)
    upper = lax.broadcasted_iota(jnp.int32, first.shape, 1) < CAP
    return (
        jnp.where(upper, first, pltpu.roll(second, 4, 1)).reshape(count, lanes),
        jnp.where(upper, pltpu.roll(first, 4, 1), second).reshape(count, lanes),
    )


def instance_rows(rows_ref):
    count = rows_ref.shape[0] // 2
    both = rows_ref[...].astype(F32).reshape(count // 8, 2, 8, WIDE)
    return swap_halves(both[:, 0].reshape(count, WIDE), both[:, 1].reshape(count, WIDE))


def gate_kernel(rows_ref, hidden_ref, weight_ref, gate_ref):
    split = instance_rows(rows_ref)
    count = rows_ref.shape[0] // 2
    folded = []
    for i in range(2):
        hidden = hidden_ref[:, 0, i].reshape(count, hidden_ref.shape[4])
        result = lax.dot_general(
            hidden, weight_ref[i], (((1,), (1,)), ((), ())), preferred_element_type=F32
        )
        product = result * split[i][:, :PIECE]
        blank = jnp.zeros((count, WIDE - PIECE), F32)
        tail = jnp.concatenate([product[:, 128:PIECE], blank], axis=1)
        folded.append(product[:, :128] + tail)
    even, odd = swap_halves(*folded)
    both = jnp.concatenate(
        [even.reshape(count // 8, 1, 8, 128), odd.reshape(count // 8, 1, 8, 128)], axis=1
    )
    both = both.reshape(count * 2 // 128, 128, 128)
    for g in range(count * 2 // 128):
        gate_ref[g] = jnp.sum(both[g].T, axis=0, keepdims=True)


def gate_parts(rows, hidden, weight):
    lines, steps, _, span, ff = hidden.shape
    dp = lines * steps
    return pl.pallas_call(
        gate_kernel,
        grid=(steps,),
        in_specs=[
            pl.BlockSpec((lines * span * 2, WIDE), lambda s: (s, 0)),
            pl.BlockSpec((lines, 1, 2, span, ff), lambda s: (0, s, 0, 0, 0)),
            pl.BlockSpec((2, PIECE, ff), lambda s: (0, 0, 0)),
        ],
        out_specs=pl.BlockSpec((lines, 1, 2 * span), lambda s: (s, 0, 0)),
        out_shape=jax.ShapeDtypeStruct((dp, 1, 2 * span), F32),
        cost_estimate=pl.CostEstimate(
            flops=4 * dp * span * PIECE * ff,
            bytes_accessed=2 * hidden.size + 2 * rows.size + 2 * weight.size,
            transcendentals=0,
        ),
        name="gate_parts",
    )(rows, hidden, weight)


def add_grad(which, rows_ref, hidden_ref, acc_ref):
    lines, span, ff = hidden_ref.shape
    grad = lax.dot_general(
        instance_rows(rows_ref)[which][:, :PIECE].astype(BF16),
        hidden_ref[...].reshape(lines * span, ff),
        (((0,), (0,)), ((), ())),
        preferred_element_type=F32,
    )

    @pl.when(pl.program_id(0) == 0)
    def _():
        acc_ref[...] = grad

    @pl.when(pl.program_id(0) != 0)
    def _():
        acc_ref[...] += grad


def hot_kernel(rows_ref, hidden_ref, hot_ref, send_ref, acc_ref):
    add_grad(0, rows_ref, hidden_ref, acc_ref)

    @pl.when(pl.program_id(0) == pl.num_programs(0) - 1)
    def _():
        hot_ref[...] = acc_ref[...]
        send_ref[...] = acc_ref[...].astype(BF16)


def cold_kernel(rows_ref, hidden_ref, out_ref, acc_ref):
    add_grad(1, rows_ref, hidden_ref, acc_ref)

    @pl.when(pl.program_id(0) == pl.num_programs(0) - 1)
    def _():
        out_ref[0] = acc_ref[...].astype(BF16)


def weight_parts(which, rows, hidden):
    lines, steps, _, span, ff = hidden.shape
    dp = lines * steps
    whole = pl.BlockSpec((PIECE, ff), lambda s: (0, 0))
    hot = which == 0
    return pl.pallas_call(
        hot_kernel if hot else cold_kernel,
        grid=(steps,),
        in_specs=[
            pl.BlockSpec((lines * span * 2, WIDE), lambda s: (s, 0)),
            pl.BlockSpec((lines, None, None, span, ff), lambda s: (0, s, which, 0, 0)),
        ],
        out_specs=[whole, whole] if hot else pl.BlockSpec((1, PIECE, ff), lambda s: (1, 0, 0)),
        out_shape=[jax.ShapeDtypeStruct((PIECE, ff), t) for t in (F32, BF16)]
        if hot
        else jax.ShapeDtypeStruct((2, PIECE, ff), BF16),
        scratch_shapes=[pltpu.VMEM((PIECE, ff), F32)],
        cost_estimate=pl.CostEstimate(
            flops=2 * dp * span * PIECE * ff,
            bytes_accessed=hidden.size + 2 * rows.size,
            transcendentals=0,
        ),
        name="hot_parts" if hot else "cold_parts",
    )(rows, hidden)


def copy_kernel(in_ref, out_ref):
    out_ref[...] = in_ref[...]


def copied(x):
    block = pl.BlockSpec((1,) + x.shape[1:], lambda s: (s, 0, 0, 0))
    return pl.pallas_call(
        copy_kernel,
        grid=x.shape[:1],
        in_specs=[block],
        out_specs=block,
        out_shape=jax.ShapeDtypeStruct(x.shape, x.dtype),
        name="copied",
    )(x)


def pair_kernel(hot_ref, other_ref, grad_ref, out_ref):
    out_ref[0] = (hot_ref[...] + other_ref[...].astype(F32)).astype(BF16)


def pair_sum(hot, other, grad):
    ff = hot.shape[1]
    whole = pl.BlockSpec((PIECE, ff), lambda s: (0, 0))
    return pl.pallas_call(
        pair_kernel,
        grid=(1,),
        in_specs=[whole, whole, pl.BlockSpec(memory_space=pl.ANY)],
        out_specs=pl.BlockSpec((1, PIECE, ff), lambda s: (0, 0, 0)),
        out_shape=jax.ShapeDtypeStruct(grad.shape, BF16),
        input_output_aliases={2: 0},
        name="pair_sum",
    )(hot, other, grad)


def total_kernel(parts_ref, out_ref):
    total = jnp.sum(parts_ref[...], axis=0)
    for e in range(out_ref.shape[0]):
        out_ref[e] = total[:, e * 2 * CAP : (e + 1) * 2 * CAP]


def gate_totals(parts, expert):
    vmem = pl.BlockSpec(memory_space=pltpu.VMEM)
    return pl.pallas_call(
        total_kernel,
        in_specs=[vmem],
        out_specs=vmem,
        out_shape=jax.ShapeDtypeStruct((expert, 1, 2 * CAP), F32),
        name="gate_totals",
    )(parts)


def pick_kernel(place_ref, ids_ref, pick_ref, gate_ref, back_ref, out_ref):
    masks, _, rank = route_masks(ids_ref, pick_ref, place_ref)
    experts = back_ref.shape[0]
    spread = (
        lax.broadcasted_iota(jnp.int32, (INSTANCES, experts), 0) // 2
        == lax.broadcasted_iota(jnp.int32, (INSTANCES, experts), 1)
    ).astype(F32)
    back = jnp.dot(
        spread,
        back_ref[...].reshape(experts, 2 * CAP),
        precision=lax.Precision.HIGHEST,
        preferred_element_type=F32,
    )
    odd = lax.broadcasted_iota(jnp.int32, (INSTANCES, 1), 0) % 2 == 1
    value = jnp.zeros((INSTANCES, TOK), F32)
    for c in range(CAP):
        column = jnp.where(odd, back[:, CAP + c : CAP + c + 1], back[:, c : c + 1])
        value = jnp.where(rank == c, jnp.broadcast_to(column, (INSTANCES, TOK)), value)
    for k in range(TOP):
        total = jnp.sum(masks[k] * value, axis=0, keepdims=True)
        low = gate_ref[k : k + 1, :].astype(BF16).astype(F32)
        out_ref[k : k + 1, :] = total / low


def pick_gates(placement, ids, pick, gates, back):
    vmem = pl.BlockSpec(memory_space=pltpu.VMEM)
    return pl.pallas_call(
        pick_kernel,
        in_specs=[pl.BlockSpec(memory_space=pltpu.SMEM)] + [vmem] * 4,
        out_specs=vmem,
        out_shape=jax.ShapeDtypeStruct((TOP, TOK), F32),
        name="pick_gates",
    )(placement, ids, pick, gates, back)


LINES = ("y", "c")
EXPERT = ("zh", "x")
GROUPS = ("zl",) + LINES
EVERY = GROUPS + EXPERT


def layer(grad_out, gate_weights, route_ids, replica_pick, placement, hidden_act, down_proj):
    dp, expert = lax.axis_size(GROUPS), lax.axis_size(EXPERT)
    ff = hidden_act.shape[4]
    local = hidden_act[0].transpose(1, 0, 2, 3).reshape(1, 2, expert * CAP, ff)
    column = lax.all_gather(local, "zl", axis=0, tiled=True)
    column = copied(column)
    hidden = lax.all_gather(column[None], LINES, axis=0, tiled=True)
    ids, pick, gates = route_ids.T, replica_pick.T, gate_weights.T
    sent = gather_rows(placement, ids, pick, gates, grad_out)
    sent = sent.reshape(dp * expert, 2 * CAP, WIDE)
    rows = lax.all_to_all(sent, EVERY, split_axis=0, concat_axis=0, tiled=True)
    rows = rows.reshape(dp * expert * 2 * CAP, WIDE)
    parts = gate_parts(rows, hidden, down_proj)
    parts = lax.all_to_all(parts, GROUPS, split_axis=0, concat_axis=0, tiled=True)
    hot, hot_sent = weight_parts(0, rows, hidden)
    half = expert // 2
    other = lax.ppermute(hot_sent, EXPERT, [(e, (e + half) % expert) for e in range(expert)])
    grad = weight_parts(1, rows, hidden)
    own = gate_totals(parts, expert)
    back = lax.all_to_all(own, EXPERT, split_axis=0, concat_axis=0, tiled=True)
    grad_gate = pick_gates(placement, ids, pick, gates, back).T
    return pair_sum(hot, other, grad), grad_gate


def solution(mesh):
    fine = jax.sharding.Mesh(mesh.devices.reshape(4, 4, 2, 4, 4), EVERY)
    token = P(EVERY, None)
    return jax.shard_map(
        layer,
        mesh=fine,
        in_specs=(
            token,
            token,
            token,
            token,
            P(),
            P(GROUPS, None, EXPERT, None, None),
            P(EXPERT, GROUPS, None),
        ),
        out_specs=(P(EXPERT, GROUPS, None), token),
        check_vma=False,
    )
```

```python
import functools
import jax
import jax.numpy as jnp
from jax import lax
from jax.experimental import pallas as pl
from jax.experimental.pallas import tpu as pltpu
from jax.sharding import PartitionSpec as P


F32 = jnp.float32
BF16 = jnp.bfloat16
INSTANCES = 32
CAP = 4
TOP = 8
TOK = 128
SLOTS = INSTANCES * CAP
PIECE = 224
WIDE = 256


def route_masks(ids_ref, pick_ref, place_ref):
    rows = lax.broadcasted_iota(jnp.int32, (INSTANCES, TOK), 0)
    place = jnp.zeros((INSTANCES, TOK), jnp.int32)
    for i in range(INSTANCES):
        place = jnp.where(rows == i, place_ref[i], place)
    single = rows % 2 == 1
    first = rows < INSTANCES // 2
    masks = []
    for k in range(TOP):
        low = jnp.broadcast_to(pick_ref[k : k + 1, :], (INSTANCES, TOK)) == 0
        serves = jnp.logical_or(single, low == first)
        same = jnp.broadcast_to(ids_ref[k : k + 1, :], (INSTANCES, TOK)) == place
        masks.append(jnp.where(jnp.logical_and(same, serves), 1.0, 0.0).astype(F32))
    taken = functools.reduce(jnp.add, masks)
    before = (
        lax.broadcasted_iota(jnp.int32, (TOK, TOK), 0)
        < lax.broadcasted_iota(jnp.int32, (TOK, TOK), 1)
    ).astype(F32)
    rank = jnp.dot(taken.astype(BF16), before.astype(BF16), preferred_element_type=F32)
    return masks, taken, rank


def gather_kernel(place_ref, ids_ref, pick_ref, gate_ref, grad_ref, out_ref, select_ref):
    @pl.when(pl.program_id(0) == 0)
    def _():
        masks, _, rank = route_masks(ids_ref, pick_ref, place_ref)
        gates = jnp.zeros((INSTANCES, TOK), F32)
        for k in range(TOP):
            low = gate_ref[k : k + 1, :].astype(BF16).astype(F32)
            gates = gates + masks[k] * jnp.broadcast_to(low, (INSTANCES, TOK))
        spread = (
            lax.broadcasted_iota(jnp.int32, (SLOTS, INSTANCES), 0) // CAP
            == lax.broadcasted_iota(jnp.int32, (SLOTS, INSTANCES), 1)
        ).astype(F32).astype(BF16)
        slot_rank = jnp.dot(spread, rank.astype(BF16), preferred_element_type=F32)
        slot_gate = jnp.dot(spread, gates.astype(BF16), preferred_element_type=F32)
        own = (lax.broadcasted_iota(jnp.int32, (SLOTS, TOK), 0) % CAP).astype(F32)
        select_ref[...] = jnp.where(slot_rank == own, slot_gate, 0.0).astype(BF16)

    rows = jnp.dot(select_ref[...], grad_ref[...], preferred_element_type=F32)
    blank = jnp.zeros((SLOTS, WIDE - PIECE), F32)
    for j in range(4):
        part = jnp.concatenate([rows[:, j * PIECE : (j + 1) * PIECE], blank], axis=1)
        out_ref[j] = part.astype(BF16)


def gather_rows(placement, ids, pick, gates, grad_out):
    width = grad_out.shape[1]
    steps = width // (4 * PIECE)
    whole = pl.BlockSpec((TOP, TOK), lambda s: (0, 0))
    return pl.pallas_call(
        gather_kernel,
        grid=(steps,),
        in_specs=[
            pl.BlockSpec(memory_space=pltpu.SMEM),
            whole,
            whole,
            whole,
            pl.BlockSpec((TOK, 4 * PIECE), lambda s: (0, s)),
        ],
        out_specs=pl.BlockSpec((4, SLOTS, WIDE), lambda s: (s, 0, 0)),
        out_shape=jax.ShapeDtypeStruct((steps * 4, SLOTS, WIDE), BF16),
        scratch_shapes=[pltpu.VMEM((SLOTS, TOK), BF16)],
        cost_estimate=pl.CostEstimate(
            flops=2 * SLOTS * TOK * width, bytes_accessed=4 * TOK * width, transcendentals=0
        ),
        name="gather_rows",
    )(placement, ids, pick, gates, grad_out)


def swap_halves(first, second):
    count, lanes = first.shape
    first, second = first.reshape(count // 8, 8, lanes), second.reshape(count // 8, 8, lanes)
    upper = lax.broadcasted_iota(jnp.int32, first.shape, 1) < CAP
    return (
        jnp.where(upper, first, pltpu.roll(second, 4, 1)).reshape(count, lanes),
        jnp.where(upper, pltpu.roll(first, 4, 1), second).reshape(count, lanes),
    )


def instance_rows(rows_ref):
    count = rows_ref.shape[0] // 2
    both = rows_ref[...].astype(F32).reshape(count // 8, 2, 8, WIDE)
    return swap_halves(both[:, 0].reshape(count, WIDE), both[:, 1].reshape(count, WIDE))


def folded_dots(rows, hidden, weight):
    result = lax.dot_general(hidden, weight, (((1,), (1,)), ((), ())), preferred_element_type=F32)
    product = result * rows[:, :PIECE]
    blank = jnp.zeros((rows.shape[0], WIDE - PIECE), F32)
    return product[:, :128] + jnp.concatenate([product[:, 128:PIECE], blank], axis=1)


def add_grad(acc_ref, rows, hidden):
    grad = lax.dot_general(
        rows[:, :PIECE].astype(BF16), hidden, (((0,), (0,)), ((), ())), preferred_element_type=F32
    )

    @pl.when(pl.program_id(0) == 0)
    def _():
        acc_ref[...] = grad

    @pl.when(pl.program_id(0) != 0)
    def _():
        acc_ref[...] += grad


def first_kernel(place_ref, rows_ref, hidden_ref, weight_ref, gate_ref, hot_ref, send_ref, acc_ref):
    lines, _, span, ff = hidden_ref.shape
    count = lines * span
    split = instance_rows(rows_ref)
    hidden = [hidden_ref[:, i].reshape(count, ff) for i in range(2)]
    add_grad(acc_ref, split[0], hidden[0])
    even, odd = swap_halves(*(folded_dots(split[i], hidden[i], weight_ref[i]) for i in range(2)))
    both = jnp.concatenate(
        [even.reshape(count // 8, 1, 8, 128), odd.reshape(count // 8, 1, 8, 128)], axis=1
    )
    both = both.reshape(count * 2 // 128, 128, 128)
    for g in range(count * 2 // 128):
        gate_ref[g] = jnp.sum(both[g].T, axis=0, keepdims=True)

    @pl.when(pl.program_id(0) == pl.num_programs(0) - 1)
    def _():
        hot_ref[...] = acc_ref[...]
        send_ref[...] = acc_ref[...].astype(BF16)


def first_parts(place, rows, hidden, weight):
    lines, steps, _, span, ff = hidden.shape
    dp = lines * steps
    whole = pl.BlockSpec((PIECE, ff), lambda s, m: (0, 0))
    return pl.pallas_call(
        first_kernel,
        grid_spec=pltpu.PrefetchScalarGridSpec(
            num_scalar_prefetch=1,
            grid=(steps,),
            in_specs=[
                pl.BlockSpec((lines * span * 2, WIDE), lambda s, m: (s, 0)),
                pl.BlockSpec(
                    (lines, None, 2, span, ff),
                    lambda s, m: (0, lax.rem(m[0] - s + steps, steps), 0, 0, 0),
                ),
                pl.BlockSpec((2, PIECE, ff), lambda s, m: (0, 0, 0)),
            ],
            out_specs=[
                pl.BlockSpec((lines, 1, 2 * span), lambda s, m: (s, 0, 0)),
                whole,
                whole,
            ],
            scratch_shapes=[pltpu.VMEM((PIECE, ff), F32)],
        ),
        out_shape=[
            jax.ShapeDtypeStruct((dp, 1, 2 * span), F32),
            jax.ShapeDtypeStruct((PIECE, ff), F32),
            jax.ShapeDtypeStruct((PIECE, ff), BF16),
        ],
        cost_estimate=pl.CostEstimate(
            flops=6 * dp * span * PIECE * ff,
            bytes_accessed=2 * hidden.size + 2 * rows.size + 2 * weight.size,
            transcendentals=0,
        ),
        name="first_parts",
    )(place, rows, hidden, weight)


def cold_kernel(place_ref, rows_ref, hidden_ref, out_ref, acc_ref):
    lines, span, ff = hidden_ref.shape
    add_grad(acc_ref, instance_rows(rows_ref)[1], hidden_ref[...].reshape(lines * span, ff))

    @pl.when(pl.program_id(0) == pl.num_programs(0) - 1)
    def _():
        out_ref[0] = acc_ref[...].astype(BF16)


def cold_parts(place, rows, hidden):
    lines, steps, _, span, ff = hidden.shape
    return pl.pallas_call(
        cold_kernel,
        grid_spec=pltpu.PrefetchScalarGridSpec(
            num_scalar_prefetch=1,
            grid=(steps,),
            in_specs=[
                pl.BlockSpec((lines * span * 2, WIDE), lambda s, m: (s, 0)),
                pl.BlockSpec(
                    (lines, None, None, span, ff),
                    lambda s, m: (0, lax.rem(m[0] - s + steps, steps), 1, 0, 0),
                ),
            ],
            out_specs=pl.BlockSpec((1, PIECE, ff), lambda s, m: (1, 0, 0)),
            scratch_shapes=[pltpu.VMEM((PIECE, ff), F32)],
        ),
        out_shape=jax.ShapeDtypeStruct((2, PIECE, ff), BF16),
        cost_estimate=pl.CostEstimate(
            flops=2 * lines * steps * span * PIECE * ff,
            bytes_accessed=hidden.size + 2 * rows.size,
            transcendentals=0,
        ),
        name="cold_parts",
    )(place, rows, hidden)


def pair_kernel(hot_ref, other_ref, grad_ref, out_ref):
    out_ref[0] = (hot_ref[...] + other_ref[...].astype(F32)).astype(BF16)


def pair_sum(hot, other, grad):
    ff = hot.shape[1]
    whole = pl.BlockSpec((PIECE, ff), lambda s: (0, 0))
    return pl.pallas_call(
        pair_kernel,
        grid=(1,),
        in_specs=[whole, whole, pl.BlockSpec(memory_space=pl.ANY)],
        out_specs=pl.BlockSpec((1, PIECE, ff), lambda s: (0, 0, 0)),
        out_shape=jax.ShapeDtypeStruct(grad.shape, BF16),
        input_output_aliases={2: 0},
        name="pair_sum",
    )(hot, other, grad)


def total_kernel(parts_ref, out_ref):
    total = jnp.sum(parts_ref[...], axis=0)
    for e in range(out_ref.shape[0]):
        out_ref[e] = total[:, e * 2 * CAP : (e + 1) * 2 * CAP]


def gate_totals(parts, expert):
    vmem = pl.BlockSpec(memory_space=pltpu.VMEM)
    return pl.pallas_call(
        total_kernel,
        in_specs=[vmem],
        out_specs=vmem,
        out_shape=jax.ShapeDtypeStruct((expert, 1, 2 * CAP), F32),
        name="gate_totals",
    )(parts)


def pick_kernel(place_ref, ids_ref, pick_ref, gate_ref, back_ref, out_ref):
    masks, _, rank = route_masks(ids_ref, pick_ref, place_ref)
    experts = back_ref.shape[0]
    spread = (
        lax.broadcasted_iota(jnp.int32, (INSTANCES, experts), 0) // 2
        == lax.broadcasted_iota(jnp.int32, (INSTANCES, experts), 1)
    ).astype(F32)
    back = jnp.dot(
        spread,
        back_ref[...].reshape(experts, 2 * CAP),
        precision=lax.Precision.HIGHEST,
        preferred_element_type=F32,
    )
    odd = lax.broadcasted_iota(jnp.int32, (INSTANCES, 1), 0) % 2 == 1
    value = jnp.zeros((INSTANCES, TOK), F32)
    for c in range(CAP):
        column = jnp.where(odd, back[:, CAP + c : CAP + c + 1], back[:, c : c + 1])
        value = jnp.where(rank == c, jnp.broadcast_to(column, (INSTANCES, TOK)), value)
    for k in range(TOP):
        total = jnp.sum(masks[k] * value, axis=0, keepdims=True)
        low = gate_ref[k : k + 1, :].astype(BF16).astype(F32)
        out_ref[k : k + 1, :] = total / low


def pick_gates(placement, ids, pick, gates, back):
    vmem = pl.BlockSpec(memory_space=pltpu.VMEM)
    return pl.pallas_call(
        pick_kernel,
        in_specs=[pl.BlockSpec(memory_space=pltpu.SMEM)] + [vmem] * 4,
        out_specs=vmem,
        out_shape=jax.ShapeDtypeStruct((TOP, TOK), F32),
        name="pick_gates",
    )(placement, ids, pick, gates, back)


LINES = ("y", "c")
EXPERT = ("zh", "x")
GROUPS = ("zl",) + LINES
EVERY = GROUPS + EXPERT


def layer(grad_out, gate_weights, route_ids, replica_pick, placement, hidden_act, down_proj):
    dp, expert = lax.axis_size(GROUPS), lax.axis_size(EXPERT)
    depth = lax.axis_size("zl")
    ff = hidden_act.shape[4]
    local = hidden_act[0].transpose(1, 0, 2, 3).reshape(1, 1, 2, expert * CAP, ff)
    column = [local] + [
        lax.ppermute(local, "zl", [(z, (z + d) % depth) for z in range(depth)])
        for d in range(1, depth)
    ]
    column = jnp.concatenate(column, axis=1)
    hidden = lax.all_gather(column, LINES, axis=0, tiled=True)
    place = lax.axis_index("zl").astype(jnp.int32).reshape(1)
    ids, pick, gates = route_ids.T, replica_pick.T, gate_weights.T
    sent = gather_rows(placement, ids, pick, gates, grad_out)
    sent = sent.reshape(dp * expert, 2 * CAP, WIDE)
    rows = lax.all_to_all(sent, EVERY, split_axis=0, concat_axis=0, tiled=True)
    rows = rows.reshape(dp * expert * 2 * CAP, WIDE)
    parts, hot, hot_sent = first_parts(place, rows, hidden, down_proj)
    parts = lax.all_to_all(parts, GROUPS, split_axis=0, concat_axis=0, tiled=True)
    half = expert // 2
    other = lax.ppermute(hot_sent, EXPERT, [(e, (e + half) % expert) for e in range(expert)])
    grad = cold_parts(place, rows, hidden)
    own = gate_totals(parts, expert)
    back = lax.all_to_all(own, EXPERT, split_axis=0, concat_axis=0, tiled=True)
    grad_gate = pick_gates(placement, ids, pick, gates, back).T
    return pair_sum(hot, other, grad), grad_gate


def solution(mesh):
    fine = jax.sharding.Mesh(mesh.devices.reshape(4, 4, 2, 4, 4), EVERY)
    token = P(EVERY, None)
    return jax.shard_map(
        layer,
        mesh=fine,
        in_specs=(
            token,
            token,
            token,
            token,
            P(),
            P(GROUPS, None, EXPERT, None, None),
            P(EXPERT, GROUPS, None),
        ),
        out_specs=(P(EXPERT, GROUPS, None), token),
        check_vma=False,
    )
```

```python
import functools
import jax
import jax.numpy as jnp
from jax import lax
from jax.experimental import pallas as pl
from jax.experimental.pallas import tpu as pltpu
from jax.sharding import PartitionSpec as P


F32 = jnp.float32
BF16 = jnp.bfloat16
INSTANCES = 32
CAP = 4
TOP = 8
TOK = 128
SLOTS = INSTANCES * CAP
PIECE = 224
WIDE = 256


def route_masks(ids_ref, pick_ref, place_ref):
    rows = lax.broadcasted_iota(jnp.int32, (INSTANCES, TOK), 0)
    place = jnp.zeros((INSTANCES, TOK), jnp.int32)
    for i in range(INSTANCES):
        place = jnp.where(rows == i, place_ref[i], place)
    single = rows % 2 == 1
    first = rows < INSTANCES // 2
    masks = []
    for k in range(TOP):
        low = jnp.broadcast_to(pick_ref[k : k + 1, :], (INSTANCES, TOK)) == 0
        serves = jnp.logical_or(single, low == first)
        same = jnp.broadcast_to(ids_ref[k : k + 1, :], (INSTANCES, TOK)) == place
        masks.append(jnp.where(jnp.logical_and(same, serves), 1.0, 0.0).astype(F32))
    taken = functools.reduce(jnp.add, masks)
    before = (
        lax.broadcasted_iota(jnp.int32, (TOK, TOK), 0)
        < lax.broadcasted_iota(jnp.int32, (TOK, TOK), 1)
    ).astype(F32)
    rank = jnp.dot(taken.astype(BF16), before.astype(BF16), preferred_element_type=F32)
    return masks, taken, rank


def gather_kernel(place_ref, ids_ref, pick_ref, gate_ref, grad_ref, out_ref, select_ref):
    @pl.when(pl.program_id(0) == 0)
    def _():
        masks, _, rank = route_masks(ids_ref, pick_ref, place_ref)
        gates = jnp.zeros((INSTANCES, TOK), F32)
        for k in range(TOP):
            low = gate_ref[k : k + 1, :].astype(BF16).astype(F32)
            gates = gates + masks[k] * jnp.broadcast_to(low, (INSTANCES, TOK))
        spread = (
            lax.broadcasted_iota(jnp.int32, (SLOTS, INSTANCES), 0) // CAP
            == lax.broadcasted_iota(jnp.int32, (SLOTS, INSTANCES), 1)
        ).astype(F32).astype(BF16)
        slot_rank = jnp.dot(spread, rank.astype(BF16), preferred_element_type=F32)
        slot_gate = jnp.dot(spread, gates.astype(BF16), preferred_element_type=F32)
        own = (lax.broadcasted_iota(jnp.int32, (SLOTS, TOK), 0) % CAP).astype(F32)
        select_ref[...] = jnp.where(slot_rank == own, slot_gate, 0.0).astype(BF16)

    rows = jnp.dot(select_ref[...], grad_ref[...], preferred_element_type=F32)
    blank = jnp.zeros((SLOTS, WIDE - PIECE), F32)
    for j in range(4):
        part = jnp.concatenate([rows[:, j * PIECE : (j + 1) * PIECE], blank], axis=1)
        out_ref[j] = part.astype(BF16)


def gather_rows(placement, ids, pick, gates, grad_out):
    width = grad_out.shape[1]
    steps = width // (4 * PIECE)
    whole = pl.BlockSpec((TOP, TOK), lambda s: (0, 0))
    return pl.pallas_call(
        gather_kernel,
        grid=(steps,),
        in_specs=[
            pl.BlockSpec(memory_space=pltpu.SMEM),
            whole,
            whole,
            whole,
            pl.BlockSpec((TOK, 4 * PIECE), lambda s: (0, s)),
        ],
        out_specs=pl.BlockSpec((4, SLOTS, WIDE), lambda s: (s, 0, 0)),
        out_shape=jax.ShapeDtypeStruct((steps * 4, SLOTS, WIDE), BF16),
        scratch_shapes=[pltpu.VMEM((SLOTS, TOK), BF16)],
        cost_estimate=pl.CostEstimate(
            flops=2 * SLOTS * TOK * width, bytes_accessed=4 * TOK * width, transcendentals=0
        ),
        name="gather_rows",
    )(placement, ids, pick, gates, grad_out)


def swap_halves(first, second):
    count, lanes = first.shape
    first, second = first.reshape(count // 8, 8, lanes), second.reshape(count // 8, 8, lanes)
    upper = lax.broadcasted_iota(jnp.int32, first.shape, 1) < CAP
    return (
        jnp.where(upper, first, pltpu.roll(second, 4, 1)).reshape(count, lanes),
        jnp.where(upper, pltpu.roll(first, 4, 1), second).reshape(count, lanes),
    )


def piece_lines(place_ref):
    lines = []
    for other in range(2):
        for d in range(4):
            y = lax.rem(place_ref[1] - d + 4, 4)
            core = place_ref[2] if other == 0 else 1 - place_ref[2]
            lines.append(y * 2 + core)
    return lines


def instance_rows(rows_ref, lines):
    span = rows_ref.shape[0] // len(lines)
    rows = [rows_ref[pl.ds(pl.multiple_of(n * span, span), span), :].astype(F32) for n in lines]
    count = rows_ref.shape[0] // 2
    both = jnp.concatenate(rows, axis=0).reshape(count // 8, 2, 8, WIDE)
    return swap_halves(both[:, 0].reshape(count, WIDE), both[:, 1].reshape(count, WIDE))


def folded_dots(rows, hidden, weight):
    result = lax.dot_general(hidden, weight, (((1,), (1,)), ((), ())), preferred_element_type=F32)
    product = result * rows[:, :PIECE]
    blank = jnp.zeros((rows.shape[0], WIDE - PIECE), F32)
    return product[:, :128] + jnp.concatenate([product[:, 128:PIECE], blank], axis=1)


def add_grad(acc_ref, rows, hidden):
    grad = lax.dot_general(
        rows[:, :PIECE].astype(BF16), hidden, (((0,), (0,)), ((), ())), preferred_element_type=F32
    )

    @pl.when(pl.program_id(0) == 0)
    def _():
        acc_ref[...] = grad

    @pl.when(pl.program_id(0) != 0)
    def _():
        acc_ref[...] += grad


def first_kernel(place_ref, rows_ref, weight_ref, *refs):
    pieces, (gate_ref, hot_ref, send_ref, acc_ref) = refs[:-4], refs[-4:]
    lines = piece_lines(place_ref)
    split = instance_rows(rows_ref, lines)
    count = rows_ref.shape[0] // 2
    hidden = [jnp.concatenate([piece[i] for piece in pieces], axis=0) for i in range(2)]
    add_grad(acc_ref, split[0], hidden[0])
    even, odd = swap_halves(*(folded_dots(split[i], hidden[i], weight_ref[i]) for i in range(2)))
    both = jnp.concatenate(
        [even.reshape(count // 8, 1, 8, 128), odd.reshape(count // 8, 1, 8, 128)], axis=1
    )
    both = both.reshape(count * 2 // 128, 128, 128)
    for g, line in enumerate(lines):
        gate_ref[line] = jnp.sum(both[g].T, axis=0, keepdims=True)

    @pl.when(pl.program_id(0) == pl.num_programs(0) - 1)
    def _():
        hot_ref[...] = acc_ref[...]
        send_ref[...] = acc_ref[...].astype(BF16)


def piece_index(s, m, instance):
    return (lax.rem(m[0] - s + 4, 4), instance, 0, 0)


def first_parts(place, rows, pieces, weight):
    steps, _, span, ff = pieces[0].shape
    lines = len(pieces)
    dp = lines * steps
    whole = pl.BlockSpec((PIECE, ff), lambda s, m: (0, 0))
    return pl.pallas_call(
        first_kernel,
        grid_spec=pltpu.PrefetchScalarGridSpec(
            num_scalar_prefetch=1,
            grid=(steps,),
            in_specs=[
                pl.BlockSpec((lines * span * 2, WIDE), lambda s, m: (s, 0)),
                pl.BlockSpec((2, PIECE, ff), lambda s, m: (0, 0, 0)),
            ]
            + [pl.BlockSpec((None, 2, span, ff), lambda s, m: piece_index(s, m, 0))] * lines,
            out_specs=[
                pl.BlockSpec((lines, 1, 2 * span), lambda s, m: (s, 0, 0)),
                whole,
                whole,
            ],
            scratch_shapes=[pltpu.VMEM((PIECE, ff), F32)],
        ),
        out_shape=[
            jax.ShapeDtypeStruct((dp, 1, 2 * span), F32),
            jax.ShapeDtypeStruct((PIECE, ff), F32),
            jax.ShapeDtypeStruct((PIECE, ff), BF16),
        ],
        cost_estimate=pl.CostEstimate(
            flops=6 * dp * span * PIECE * ff,
            bytes_accessed=4 * dp * span * ff + 2 * rows.size + 2 * weight.size,
            transcendentals=0,
        ),
        name="first_parts",
    )(place, rows, weight, *pieces)


def cold_kernel(place_ref, rows_ref, *refs):
    pieces, (out_ref, acc_ref) = refs[:-2], refs[-2:]
    hidden = jnp.concatenate([piece[...] for piece in pieces], axis=0)
    add_grad(acc_ref, instance_rows(rows_ref, piece_lines(place_ref))[1], hidden)

    @pl.when(pl.program_id(0) == pl.num_programs(0) - 1)
    def _():
        out_ref[0] = acc_ref[...].astype(BF16)


def cold_parts(place, rows, pieces):
    steps, _, span, ff = pieces[0].shape
    lines = len(pieces)
    return pl.pallas_call(
        cold_kernel,
        grid_spec=pltpu.PrefetchScalarGridSpec(
            num_scalar_prefetch=1,
            grid=(steps,),
            in_specs=[pl.BlockSpec((lines * span * 2, WIDE), lambda s, m: (s, 0))]
            + [pl.BlockSpec((None, None, span, ff), lambda s, m: piece_index(s, m, 1))] * lines,
            out_specs=pl.BlockSpec((1, PIECE, ff), lambda s, m: (1, 0, 0)),
            scratch_shapes=[pltpu.VMEM((PIECE, ff), F32)],
        ),
        out_shape=jax.ShapeDtypeStruct((2, PIECE, ff), BF16),
        cost_estimate=pl.CostEstimate(
            flops=2 * lines * steps * span * PIECE * ff,
            bytes_accessed=2 * lines * steps * span * ff + 2 * rows.size,
            transcendentals=0,
        ),
        name="cold_parts",
    )(place, rows, *pieces)


def pair_kernel(hot_ref, other_ref, grad_ref, out_ref):
    out_ref[0] = (hot_ref[...] + other_ref[...].astype(F32)).astype(BF16)


def pair_sum(hot, other, grad):
    ff = hot.shape[1]
    whole = pl.BlockSpec((PIECE, ff), lambda s: (0, 0))
    return pl.pallas_call(
        pair_kernel,
        grid=(1,),
        in_specs=[whole, whole, pl.BlockSpec(memory_space=pl.ANY)],
        out_specs=pl.BlockSpec((1, PIECE, ff), lambda s: (0, 0, 0)),
        out_shape=jax.ShapeDtypeStruct(grad.shape, BF16),
        input_output_aliases={2: 0},
        name="pair_sum",
    )(hot, other, grad)


def total_kernel(parts_ref, out_ref):
    total = jnp.sum(parts_ref[...], axis=0)
    for e in range(out_ref.shape[0]):
        out_ref[e] = total[:, e * 2 * CAP : (e + 1) * 2 * CAP]


def gate_totals(parts, expert):
    vmem = pl.BlockSpec(memory_space=pltpu.VMEM)
    return pl.pallas_call(
        total_kernel,
        in_specs=[vmem],
        out_specs=vmem,
        out_shape=jax.ShapeDtypeStruct((expert, 1, 2 * CAP), F32),
        name="gate_totals",
    )(parts)


def pick_kernel(place_ref, ids_ref, pick_ref, gate_ref, back_ref, out_ref):
    masks, _, rank = route_masks(ids_ref, pick_ref, place_ref)
    experts = back_ref.shape[0]
    spread = (
        lax.broadcasted_iota(jnp.int32, (INSTANCES, experts), 0) // 2
        == lax.broadcasted_iota(jnp.int32, (INSTANCES, experts), 1)
    ).astype(F32)
    back = jnp.dot(
        spread,
        back_ref[...].reshape(experts, 2 * CAP),
        precision=lax.Precision.HIGHEST,
        preferred_element_type=F32,
    )
    odd = lax.broadcasted_iota(jnp.int32, (INSTANCES, 1), 0) % 2 == 1
    value = jnp.zeros((INSTANCES, TOK), F32)
    for c in range(CAP):
        column = jnp.where(odd, back[:, CAP + c : CAP + c + 1], back[:, c : c + 1])
        value = jnp.where(rank == c, jnp.broadcast_to(column, (INSTANCES, TOK)), value)
    for k in range(TOP):
        total = jnp.sum(masks[k] * value, axis=0, keepdims=True)
        low = gate_ref[k : k + 1, :].astype(BF16).astype(F32)
        out_ref[k : k + 1, :] = total / low


def pick_gates(placement, ids, pick, gates, back):
    vmem = pl.BlockSpec(memory_space=pltpu.VMEM)
    return pl.pallas_call(
        pick_kernel,
        in_specs=[pl.BlockSpec(memory_space=pltpu.SMEM)] + [vmem] * 4,
        out_specs=vmem,
        out_shape=jax.ShapeDtypeStruct((TOP, TOK), F32),
        name="pick_gates",
    )(placement, ids, pick, gates, back)


LINES = ("y", "c")
EXPERT = ("zh", "x")
GROUPS = ("zl",) + LINES
EVERY = GROUPS + EXPERT


def layer(grad_out, gate_weights, route_ids, replica_pick, placement, hidden_act, down_proj):
    dp, expert = lax.axis_size(GROUPS), lax.axis_size(EXPERT)
    depth = lax.axis_size("zl")
    ff = hidden_act.shape[4]
    local = hidden_act[0].transpose(1, 0, 2, 3).reshape(1, 2, expert * CAP, ff)
    column = [local] + [
        lax.ppermute(local, "zl", [(z, (z + d) % depth) for z in range(depth)])
        for d in range(1, depth)
    ]
    column = jnp.concatenate(column, axis=0)
    pieces = [column]
    for d in range(1, lax.axis_size("y")):
        pieces.append(lax.ppermute(column, "y", [(y, (y + d) % 4) for y in range(4)]))
    pieces = pieces + [lax.ppermute(piece, "c", [(0, 1), (1, 0)]) for piece in pieces]
    place = jnp.stack([lax.axis_index(axis) for axis in GROUPS]).astype(jnp.int32)
    ids, pick, gates = route_ids.T, replica_pick.T, gate_weights.T
    sent = gather_rows(placement, ids, pick, gates, grad_out)
    sent = sent.reshape(dp * expert, 2 * CAP, WIDE)
    rows = lax.all_to_all(sent, EVERY, split_axis=0, concat_axis=0, tiled=True)
    rows = rows.reshape(dp * expert * 2 * CAP, WIDE)
    parts, hot, hot_sent = first_parts(place, rows, pieces, down_proj)
    parts = lax.all_to_all(parts, GROUPS, split_axis=0, concat_axis=0, tiled=True)
    half = expert // 2
    other = lax.ppermute(hot_sent, EXPERT, [(e, (e + half) % expert) for e in range(expert)])
    grad = cold_parts(place, rows, pieces)
    own = gate_totals(parts, expert)
    back = lax.all_to_all(own, EXPERT, split_axis=0, concat_axis=0, tiled=True)
    grad_gate = pick_gates(placement, ids, pick, gates, back).T
    return pair_sum(hot, other, grad), grad_gate


def solution(mesh):
    fine = jax.sharding.Mesh(mesh.devices.reshape(4, 4, 2, 4, 4), EVERY)
    token = P(EVERY, None)
    return jax.shard_map(
        layer,
        mesh=fine,
        in_specs=(
            token,
            token,
            token,
            token,
            P(),
            P(GROUPS, None, EXPERT, None, None),
            P(EXPERT, GROUPS, None),
        ),
        out_specs=(P(EXPERT, GROUPS, None), token),
        check_vma=False,
    )
```

```python
import functools
import jax
import jax.numpy as jnp
from jax import lax
from jax.experimental import pallas as pl
from jax.experimental.pallas import tpu as pltpu
from jax.sharding import PartitionSpec as P


F32 = jnp.float32
BF16 = jnp.bfloat16
INSTANCES = 32
CAP = 4
TOP = 8
TOK = 128
SLOTS = INSTANCES * CAP
PIECE = 224
WIDE = 256


def route_masks(ids_ref, pick_ref, place_ref):
    rows = lax.broadcasted_iota(jnp.int32, (INSTANCES, TOK), 0)
    place = jnp.zeros((INSTANCES, TOK), jnp.int32)
    for i in range(INSTANCES):
        place = jnp.where(rows == i, place_ref[i], place)
    single = rows % 2 == 1
    first = rows < INSTANCES // 2
    masks = []
    for k in range(TOP):
        low = jnp.broadcast_to(pick_ref[k : k + 1, :], (INSTANCES, TOK)) == 0
        serves = jnp.logical_or(single, low == first)
        same = jnp.broadcast_to(ids_ref[k : k + 1, :], (INSTANCES, TOK)) == place
        masks.append(jnp.where(jnp.logical_and(same, serves), 1.0, 0.0).astype(F32))
    taken = functools.reduce(jnp.add, masks)
    before = (
        lax.broadcasted_iota(jnp.int32, (TOK, TOK), 0)
        < lax.broadcasted_iota(jnp.int32, (TOK, TOK), 1)
    ).astype(F32)
    rank = jnp.dot(taken.astype(BF16), before.astype(BF16), preferred_element_type=F32)
    return masks, taken, rank


def gather_kernel(place_ref, ids_ref, pick_ref, gate_ref, grad_ref, out_ref, select_ref):
    @pl.when(pl.program_id(0) == 0)
    def _():
        masks, _, rank = route_masks(ids_ref, pick_ref, place_ref)
        gates = jnp.zeros((INSTANCES, TOK), F32)
        for k in range(TOP):
            low = gate_ref[k : k + 1, :].astype(BF16).astype(F32)
            gates = gates + masks[k] * jnp.broadcast_to(low, (INSTANCES, TOK))
        spread = (
            lax.broadcasted_iota(jnp.int32, (SLOTS, INSTANCES), 0) // CAP
            == lax.broadcasted_iota(jnp.int32, (SLOTS, INSTANCES), 1)
        ).astype(F32).astype(BF16)
        slot_rank = jnp.dot(spread, rank.astype(BF16), preferred_element_type=F32)
        slot_gate = jnp.dot(spread, gates.astype(BF16), preferred_element_type=F32)
        own = (lax.broadcasted_iota(jnp.int32, (SLOTS, TOK), 0) % CAP).astype(F32)
        select_ref[...] = jnp.where(slot_rank == own, slot_gate, 0.0).astype(BF16)

    rows = jnp.dot(select_ref[...], grad_ref[...], preferred_element_type=F32)
    blank = jnp.zeros((SLOTS, WIDE - PIECE), F32)
    for j in range(4):
        part = jnp.concatenate([rows[:, j * PIECE : (j + 1) * PIECE], blank], axis=1)
        out_ref[j] = part.astype(BF16)


def gather_rows(placement, ids, pick, gates, grad_out):
    width = grad_out.shape[1]
    steps = width // (4 * PIECE)
    whole = pl.BlockSpec((TOP, TOK), lambda s: (0, 0))
    return pl.pallas_call(
        gather_kernel,
        grid=(steps,),
        in_specs=[
            pl.BlockSpec(memory_space=pltpu.SMEM),
            whole,
            whole,
            whole,
            pl.BlockSpec((TOK, 4 * PIECE), lambda s: (0, s)),
        ],
        out_specs=pl.BlockSpec((4, SLOTS, WIDE), lambda s: (s, 0, 0)),
        out_shape=jax.ShapeDtypeStruct((steps * 4, SLOTS, WIDE), BF16),
        scratch_shapes=[pltpu.VMEM((SLOTS, TOK), BF16)],
        cost_estimate=pl.CostEstimate(
            flops=2 * SLOTS * TOK * width, bytes_accessed=4 * TOK * width, transcendentals=0
        ),
        name="gather_rows",
    )(placement, ids, pick, gates, grad_out)


def swap_halves(first, second):
    count, lanes = first.shape
    first, second = first.reshape(count // 8, 8, lanes), second.reshape(count // 8, 8, lanes)
    upper = lax.broadcasted_iota(jnp.int32, first.shape, 1) < CAP
    return (
        jnp.where(upper, first, pltpu.roll(second, 4, 1)).reshape(count, lanes),
        jnp.where(upper, pltpu.roll(first, 4, 1), second).reshape(count, lanes),
    )


def piece_lines(place_ref):
    lines = []
    for other in range(2):
        for d in range(4):
            y = lax.rem(place_ref[1] - d + 4, 4)
            core = place_ref[2] if other == 0 else 1 - place_ref[2]
            lines.append(y * 2 + core)
    return lines


def instance_rows(rows_ref, lines):
    span = rows_ref.shape[0] // len(lines)
    rows = [rows_ref[pl.ds(pl.multiple_of(n * span, span), span), :].astype(F32) for n in lines]
    count = rows_ref.shape[0] // 2
    both = jnp.concatenate(rows, axis=0).reshape(count // 8, 2, 8, WIDE)
    return swap_halves(both[:, 0].reshape(count, WIDE), both[:, 1].reshape(count, WIDE))


def folded_dots(rows, hidden, weight):
    result = lax.dot_general(hidden, weight, (((1,), (1,)), ((), ())), preferred_element_type=F32)
    product = result * rows[:, :PIECE]
    blank = jnp.zeros((rows.shape[0], WIDE - PIECE), F32)
    return product[:, :128] + jnp.concatenate([product[:, 128:PIECE], blank], axis=1)


def add_grad(acc_ref, rows, hidden):
    grad = lax.dot_general(
        rows[:, :PIECE].astype(BF16), hidden, (((0,), (0,)), ((), ())), preferred_element_type=F32
    )

    @pl.when(pl.program_id(0) == 0)
    def _():
        acc_ref[...] = grad

    @pl.when(pl.program_id(0) != 0)
    def _():
        acc_ref[...] += grad


def gate_kernel(place_ref, rows_ref, weight_ref, *refs):
    pieces, gate_ref = refs[:-1], refs[-1]
    lines = piece_lines(place_ref)
    split = instance_rows(rows_ref, lines)
    count = rows_ref.shape[0] // 2
    hidden = [jnp.concatenate([piece[i] for piece in pieces], axis=0) for i in range(2)]
    even, odd = swap_halves(*(folded_dots(split[i], hidden[i], weight_ref[i]) for i in range(2)))
    both = jnp.concatenate(
        [even.reshape(count // 8, 1, 8, 128), odd.reshape(count // 8, 1, 8, 128)], axis=1
    )
    both = both.reshape(count * 2 // 128, 128, 128)
    for g, line in enumerate(lines):
        gate_ref[line, 0] = jnp.sum(both[g].T, axis=0, keepdims=True)


def hot_kernel(place_ref, rows_ref, *refs):
    pieces, (hot_ref, send_ref, acc_ref) = refs[:-3], refs[-3:]
    hidden = jnp.concatenate([piece[...] for piece in pieces], axis=0)
    add_grad(acc_ref, instance_rows(rows_ref, piece_lines(place_ref))[0], hidden)

    @pl.when(pl.program_id(0) == pl.num_programs(0) - 1)
    def _():
        hot_ref[...] = acc_ref[...]
        send_ref[...] = acc_ref[...].astype(BF16)


def cold_kernel(place_ref, rows_ref, *refs):
    pieces, (out_ref, acc_ref) = refs[:-2], refs[-2:]
    hidden = jnp.concatenate([piece[...] for piece in pieces], axis=0)
    add_grad(acc_ref, instance_rows(rows_ref, piece_lines(place_ref))[1], hidden)

    @pl.when(pl.program_id(0) == pl.num_programs(0) - 1)
    def _():
        out_ref[0] = acc_ref[...].astype(BF16)


def piece_index(s, m, instance):
    return (lax.rem(m[0] - s + 4, 4), instance, 0, 0)


def gate_parts(place, rows, pieces, weight):
    steps, _, span, ff = pieces[0].shape
    lines = len(pieces)
    return pl.pallas_call(
        gate_kernel,
        grid_spec=pltpu.PrefetchScalarGridSpec(
            num_scalar_prefetch=1,
            grid=(steps,),
            in_specs=[
                pl.BlockSpec((lines * span * 2, WIDE), lambda s, m: (s, 0)),
                pl.BlockSpec((2, PIECE, ff), lambda s, m: (0, 0, 0)),
            ]
            + [pl.BlockSpec((None, 2, span, ff), lambda s, m: piece_index(s, m, 0))] * lines,
            out_specs=pl.BlockSpec((lines, 1, 1, 2 * span), lambda s, m: (0, s, 0, 0)),
        ),
        out_shape=jax.ShapeDtypeStruct((lines, steps, 1, 2 * span), F32),
        cost_estimate=pl.CostEstimate(
            flops=4 * lines * steps * span * PIECE * ff,
            bytes_accessed=4 * lines * steps * span * ff + 2 * rows.size + 2 * weight.size,
            transcendentals=0,
        ),
        name="gate_parts",
    )(place, rows, weight, *pieces)


def weight_parts(which, place, rows, pieces):
    steps, _, span, ff = pieces[0].shape
    lines = len(pieces)
    hot = which == 0
    whole = pl.BlockSpec((PIECE, ff), lambda s, m: (0, 0))
    half = pl.BlockSpec((1, PIECE, ff), lambda s, m: (1, 0, 0))
    return pl.pallas_call(
        hot_kernel if hot else cold_kernel,
        grid_spec=pltpu.PrefetchScalarGridSpec(
            num_scalar_prefetch=1,
            grid=(steps,),
            in_specs=[pl.BlockSpec((lines * span * 2, WIDE), lambda s, m: (s, 0))]
            + [pl.BlockSpec((None, None, span, ff), lambda s, m: piece_index(s, m, which))] * lines,
            out_specs=[whole, whole] if hot else half,
            scratch_shapes=[pltpu.VMEM((PIECE, ff), F32)],
        ),
        out_shape=[jax.ShapeDtypeStruct((PIECE, ff), t) for t in (F32, BF16)]
        if hot
        else jax.ShapeDtypeStruct((2, PIECE, ff), BF16),
        cost_estimate=pl.CostEstimate(
            flops=2 * lines * steps * span * PIECE * ff,
            bytes_accessed=2 * lines * steps * span * ff + 2 * rows.size,
            transcendentals=0,
        ),
        name="hot_parts" if hot else "cold_parts",
    )(place, rows, *pieces)


def pair_kernel(hot_ref, other_ref, grad_ref, out_ref):
    out_ref[0] = (hot_ref[...] + other_ref[...].astype(F32)).astype(BF16)


def pair_sum(hot, other, grad):
    ff = hot.shape[1]
    whole = pl.BlockSpec((PIECE, ff), lambda s: (0, 0))
    return pl.pallas_call(
        pair_kernel,
        grid=(1,),
        in_specs=[whole, whole, pl.BlockSpec(memory_space=pl.ANY)],
        out_specs=pl.BlockSpec((1, PIECE, ff), lambda s: (0, 0, 0)),
        out_shape=jax.ShapeDtypeStruct(grad.shape, BF16),
        input_output_aliases={2: 0},
        name="pair_sum",
    )(hot, other, grad)


def total_kernel(parts_ref, out_ref):
    steps = parts_ref.shape[1]
    experts = out_ref.shape[0] // steps
    total = jnp.sum(parts_ref[...], axis=0)
    for z in range(steps):
        for e in range(experts):
            out_ref[z * experts + e] = total[z, :, e * 2 * CAP : (e + 1) * 2 * CAP]


def gate_totals(parts, expert):
    vmem = pl.BlockSpec(memory_space=pltpu.VMEM)
    return pl.pallas_call(
        total_kernel,
        in_specs=[vmem],
        out_specs=vmem,
        out_shape=jax.ShapeDtypeStruct((parts.shape[1] * expert, 1, 2 * CAP), F32),
        name="gate_totals",
    )(parts)


def pick_kernel(place_ref, ids_ref, pick_ref, gate_ref, back_ref, out_ref):
    masks, _, rank = route_masks(ids_ref, pick_ref, place_ref)
    parts = back_ref.shape[0]
    spread = (
        lax.broadcasted_iota(jnp.int32, (INSTANCES, parts), 0) // 2
        == lax.broadcasted_iota(jnp.int32, (INSTANCES, parts), 1) % (INSTANCES // 2)
    ).astype(F32)
    back = jnp.dot(
        spread,
        back_ref[...].reshape(parts, 2 * CAP),
        precision=lax.Precision.HIGHEST,
        preferred_element_type=F32,
    )
    odd = lax.broadcasted_iota(jnp.int32, (INSTANCES, 1), 0) % 2 == 1
    value = jnp.zeros((INSTANCES, TOK), F32)
    for c in range(CAP):
        column = jnp.where(odd, back[:, CAP + c : CAP + c + 1], back[:, c : c + 1])
        value = jnp.where(rank == c, jnp.broadcast_to(column, (INSTANCES, TOK)), value)
    for k in range(TOP):
        total = jnp.sum(masks[k] * value, axis=0, keepdims=True)
        low = gate_ref[k : k + 1, :].astype(BF16).astype(F32)
        out_ref[k : k + 1, :] = total / low


def pick_gates(placement, ids, pick, gates, back):
    vmem = pl.BlockSpec(memory_space=pltpu.VMEM)
    return pl.pallas_call(
        pick_kernel,
        in_specs=[pl.BlockSpec(memory_space=pltpu.SMEM)] + [vmem] * 4,
        out_specs=vmem,
        out_shape=jax.ShapeDtypeStruct((TOP, TOK), F32),
        name="pick_gates",
    )(placement, ids, pick, gates, back)


LINES = ("y", "c")
EXPERT = ("zh", "x")
GROUPS = ("zl",) + LINES
EVERY = GROUPS + EXPERT


def layer(grad_out, gate_weights, route_ids, replica_pick, placement, hidden_act, down_proj):
    dp, expert = lax.axis_size(GROUPS), lax.axis_size(EXPERT)
    depth = lax.axis_size("zl")
    ff = hidden_act.shape[4]
    local = hidden_act[0].transpose(1, 0, 2, 3).reshape(1, 2, expert * CAP, ff)
    column = [local] + [
        lax.ppermute(local, "zl", [(z, (z + d) % depth) for z in range(depth)])
        for d in range(1, depth)
    ]
    column = jnp.concatenate(column, axis=0)
    pieces = [column]
    for d in range(1, lax.axis_size("y")):
        pieces.append(lax.ppermute(column, "y", [(y, (y + d) % 4) for y in range(4)]))
    pieces = pieces + [lax.ppermute(piece, "c", [(0, 1), (1, 0)]) for piece in pieces]
    place = jnp.stack([lax.axis_index(axis) for axis in GROUPS]).astype(jnp.int32)
    ids, pick, gates = route_ids.T, replica_pick.T, gate_weights.T
    sent = gather_rows(placement, ids, pick, gates, grad_out)
    sent = sent.reshape(dp * expert, 2 * CAP, WIDE)
    rows = lax.all_to_all(sent, EVERY, split_axis=0, concat_axis=0, tiled=True)
    rows = rows.reshape(dp * expert * 2 * CAP, WIDE)
    hot, hot_sent = weight_parts(0, place, rows, pieces)
    half = expert // 2
    other = lax.ppermute(hot_sent, EXPERT, [(e, (e + half) % expert) for e in range(expert)])
    parts = gate_parts(place, rows, pieces, down_proj)
    parts = lax.all_to_all(parts, LINES, split_axis=0, concat_axis=0, tiled=True)
    grad = weight_parts(1, place, rows, pieces)
    own = gate_totals(parts, expert)
    back = lax.all_to_all(own, ("zl",) + EXPERT, split_axis=0, concat_axis=0, tiled=True)
    grad_gate = pick_gates(placement, ids, pick, gates, back).T
    return pair_sum(hot, other, grad), grad_gate


def solution(mesh):
    fine = jax.sharding.Mesh(mesh.devices.reshape(4, 4, 2, 4, 4), EVERY)
    token = P(EVERY, None)
    return jax.shard_map(
        layer,
        mesh=fine,
        in_specs=(
            token,
            token,
            token,
            token,
            P(),
            P(GROUPS, None, EXPERT, None, None),
            P(EXPERT, GROUPS, None),
        ),
        out_specs=(P(EXPERT, GROUPS, None), token),
        check_vma=False,
    )
```

```python
import functools
import jax
import jax.numpy as jnp
from jax import lax
from jax.experimental import pallas as pl
from jax.experimental.pallas import tpu as pltpu
from jax.sharding import PartitionSpec as P


F32 = jnp.float32
BF16 = jnp.bfloat16
INSTANCES = 32
CAP = 4
TOP = 8
TOK = 128
SLOTS = INSTANCES * CAP
PIECE = 224
WIDE = 256


def route_masks(ids_ref, pick_ref, place_ref):
    rows = lax.broadcasted_iota(jnp.int32, (INSTANCES, TOK), 0)
    place = jnp.zeros((INSTANCES, TOK), jnp.int32)
    for i in range(INSTANCES):
        place = jnp.where(rows == i, place_ref[i], place)
    single = rows % 2 == 1
    first = rows < INSTANCES // 2
    masks = []
    for k in range(TOP):
        low = jnp.broadcast_to(pick_ref[k : k + 1, :], (INSTANCES, TOK)) == 0
        serves = jnp.logical_or(single, low == first)
        same = jnp.broadcast_to(ids_ref[k : k + 1, :], (INSTANCES, TOK)) == place
        masks.append(jnp.where(jnp.logical_and(same, serves), 1.0, 0.0).astype(F32))
    taken = functools.reduce(jnp.add, masks)
    before = (
        lax.broadcasted_iota(jnp.int32, (TOK, TOK), 0)
        < lax.broadcasted_iota(jnp.int32, (TOK, TOK), 1)
    ).astype(F32)
    rank = jnp.dot(taken.astype(BF16), before.astype(BF16), preferred_element_type=F32)
    return masks, taken, rank


def gather_kernel(place_ref, ids_ref, pick_ref, gate_ref, grad_ref, out_ref, select_ref):
    @pl.when(pl.program_id(0) == 0)
    def _():
        masks, _, rank = route_masks(ids_ref, pick_ref, place_ref)
        gates = jnp.zeros((INSTANCES, TOK), F32)
        for k in range(TOP):
            low = gate_ref[k : k + 1, :].astype(BF16).astype(F32)
            gates = gates + masks[k] * jnp.broadcast_to(low, (INSTANCES, TOK))
        spread = (
            lax.broadcasted_iota(jnp.int32, (SLOTS, INSTANCES), 0) // CAP
            == lax.broadcasted_iota(jnp.int32, (SLOTS, INSTANCES), 1)
        ).astype(F32).astype(BF16)
        slot_rank = jnp.dot(spread, rank.astype(BF16), preferred_element_type=F32)
        slot_gate = jnp.dot(spread, gates.astype(BF16), preferred_element_type=F32)
        own = (lax.broadcasted_iota(jnp.int32, (SLOTS, TOK), 0) % CAP).astype(F32)
        select_ref[...] = jnp.where(slot_rank == own, slot_gate, 0.0).astype(BF16)

    rows = jnp.dot(select_ref[...], grad_ref[...], preferred_element_type=F32)
    blank = jnp.zeros((SLOTS, WIDE - PIECE), F32)
    for j in range(out_ref.shape[0]):
        part = jnp.concatenate([rows[:, j * PIECE : (j + 1) * PIECE], blank], axis=1)
        out_ref[j] = part.astype(BF16)


def gather_rows(placement, ids, pick, gates, grad_out):
    width = grad_out.shape[1]
    per = 8
    steps = width // (per * PIECE)
    whole = pl.BlockSpec((TOP, TOK), lambda s: (0, 0))
    return pl.pallas_call(
        gather_kernel,
        grid=(steps,),
        in_specs=[
            pl.BlockSpec(memory_space=pltpu.SMEM),
            whole,
            whole,
            whole,
            pl.BlockSpec((TOK, per * PIECE), lambda s: (0, s)),
        ],
        out_specs=pl.BlockSpec((per, SLOTS, WIDE), lambda s: (s, 0, 0)),
        out_shape=jax.ShapeDtypeStruct((steps * per, SLOTS, WIDE), BF16),
        scratch_shapes=[pltpu.VMEM((SLOTS, TOK), BF16)],
        cost_estimate=pl.CostEstimate(
            flops=2 * SLOTS * TOK * width, bytes_accessed=4 * TOK * width, transcendentals=0
        ),
        name="gather_rows",
    )(placement, ids, pick, gates, grad_out)


def swap_halves(first, second):
    count, lanes = first.shape
    first, second = first.reshape(count // 8, 8, lanes), second.reshape(count // 8, 8, lanes)
    upper = lax.broadcasted_iota(jnp.int32, first.shape, 1) < CAP
    return (
        jnp.where(upper, first, pltpu.roll(second, 4, 1)).reshape(count, lanes),
        jnp.where(upper, pltpu.roll(first, 4, 1), second).reshape(count, lanes),
    )


def piece_lines(place_ref):
    lines = []
    for other in range(2):
        for d in range(4):
            y = lax.rem(place_ref[1] - d + 4, 4)
            core = place_ref[2] if other == 0 else 1 - place_ref[2]
            lines.append(y * 2 + core)
    return lines


def instance_rows(rows_ref, lines):
    span = rows_ref.shape[0] // len(lines)
    rows = [rows_ref[pl.ds(pl.multiple_of(n * span, span), span), :].astype(F32) for n in lines]
    count = rows_ref.shape[0] // 2
    both = jnp.concatenate(rows, axis=0).reshape(count // 8, 2, 8, WIDE)
    return swap_halves(both[:, 0].reshape(count, WIDE), both[:, 1].reshape(count, WIDE))


def folded_dots(rows, hidden, weight):
    result = lax.dot_general(hidden, weight, (((1,), (1,)), ((), ())), preferred_element_type=F32)
    product = result * rows[:, :PIECE]
    blank = jnp.zeros((rows.shape[0], WIDE - PIECE), F32)
    return product[:, :128] + jnp.concatenate([product[:, 128:PIECE], blank], axis=1)


def add_grad(acc_ref, rows, hidden):
    grad = lax.dot_general(
        rows[:, :PIECE].astype(BF16), hidden, (((0,), (0,)), ((), ())), preferred_element_type=F32
    )

    @pl.when(pl.program_id(0) == 0)
    def _():
        acc_ref[...] = grad

    @pl.when(pl.program_id(0) != 0)
    def _():
        acc_ref[...] += grad


def gate_kernel(place_ref, rows_ref, weight_ref, *refs):
    pieces, gate_ref = refs[:-1], refs[-1]
    lines = piece_lines(place_ref)
    split = instance_rows(rows_ref, lines)
    count = rows_ref.shape[0] // 2
    hidden = [jnp.concatenate([piece[i] for piece in pieces], axis=0) for i in range(2)]
    even, odd = swap_halves(*(folded_dots(split[i], hidden[i], weight_ref[i]) for i in range(2)))
    both = jnp.concatenate(
        [even.reshape(count // 8, 1, 8, 128), odd.reshape(count // 8, 1, 8, 128)], axis=1
    )
    both = both.reshape(count * 2 // 128, 128, 128)
    for g, line in enumerate(lines):
        gate_ref[line, 0] = jnp.sum(both[g].T, axis=0, keepdims=True)


def hot_kernel(place_ref, rows_ref, *refs):
    pieces, (hot_ref, send_ref, acc_ref) = refs[:-3], refs[-3:]
    hidden = jnp.concatenate([piece[...] for piece in pieces], axis=0)
    add_grad(acc_ref, instance_rows(rows_ref, piece_lines(place_ref))[0], hidden)

    @pl.when(pl.program_id(0) == pl.num_programs(0) - 1)
    def _():
        hot_ref[...] = acc_ref[...]
        send_ref[...] = acc_ref[...].astype(BF16)


def cold_kernel(place_ref, rows_ref, *refs):
    pieces, (out_ref, acc_ref) = refs[:-2], refs[-2:]
    hidden = jnp.concatenate([piece[...] for piece in pieces], axis=0)
    add_grad(acc_ref, instance_rows(rows_ref, piece_lines(place_ref))[1], hidden)

    @pl.when(pl.program_id(0) == pl.num_programs(0) - 1)
    def _():
        out_ref[0] = acc_ref[...].astype(BF16)


def piece_index(s, m, instance):
    return (lax.rem(m[0] - s + 4, 4), instance, 0, 0)


def gate_parts(place, rows, pieces, weight):
    steps, _, span, ff = pieces[0].shape
    lines = len(pieces)
    return pl.pallas_call(
        gate_kernel,
        grid_spec=pltpu.PrefetchScalarGridSpec(
            num_scalar_prefetch=1,
            grid=(steps,),
            in_specs=[
                pl.BlockSpec((lines * span * 2, WIDE), lambda s, m: (s, 0)),
                pl.BlockSpec((2, PIECE, ff), lambda s, m: (0, 0, 0)),
            ]
            + [pl.BlockSpec((None, 2, span, ff), lambda s, m: piece_index(s, m, 0))] * lines,
            out_specs=pl.BlockSpec((lines, 1, 1, 2 * span), lambda s, m: (0, s, 0, 0)),
        ),
        out_shape=jax.ShapeDtypeStruct((lines, steps, 1, 2 * span), F32),
        cost_estimate=pl.CostEstimate(
            flops=4 * lines * steps * span * PIECE * ff,
            bytes_accessed=4 * lines * steps * span * ff + 2 * rows.size + 2 * weight.size,
            transcendentals=0,
        ),
        name="gate_parts",
    )(place, rows, weight, *pieces)


def weight_parts(which, place, rows, pieces):
    steps, _, span, ff = pieces[0].shape
    lines = len(pieces)
    hot = which == 0
    whole = pl.BlockSpec((PIECE, ff), lambda s, m: (0, 0))
    half = pl.BlockSpec((1, PIECE, ff), lambda s, m: (1, 0, 0))
    return pl.pallas_call(
        hot_kernel if hot else cold_kernel,
        grid_spec=pltpu.PrefetchScalarGridSpec(
            num_scalar_prefetch=1,
            grid=(steps,),
            in_specs=[pl.BlockSpec((lines * span * 2, WIDE), lambda s, m: (s, 0))]
            + [pl.BlockSpec((None, None, span, ff), lambda s, m: piece_index(s, m, which))] * lines,
            out_specs=[whole, whole] if hot else half,
            scratch_shapes=[pltpu.VMEM((PIECE, ff), F32)],
        ),
        out_shape=[jax.ShapeDtypeStruct((PIECE, ff), t) for t in (F32, BF16)]
        if hot
        else jax.ShapeDtypeStruct((2, PIECE, ff), BF16),
        cost_estimate=pl.CostEstimate(
            flops=2 * lines * steps * span * PIECE * ff,
            bytes_accessed=2 * lines * steps * span * ff + 2 * rows.size,
            transcendentals=0,
        ),
        name="hot_parts" if hot else "cold_parts",
    )(place, rows, *pieces)


def total_kernel(parts_ref, out_ref):
    steps = parts_ref.shape[1]
    experts = out_ref.shape[0] // steps
    total = jnp.sum(parts_ref[...], axis=0)
    for z in range(steps):
        for e in range(experts):
            out_ref[z * experts + e] = total[z, :, e * 2 * CAP : (e + 1) * 2 * CAP]


def gate_totals(parts, expert):
    vmem = pl.BlockSpec(memory_space=pltpu.VMEM)
    return pl.pallas_call(
        total_kernel,
        in_specs=[vmem],
        out_specs=vmem,
        out_shape=jax.ShapeDtypeStruct((parts.shape[1] * expert, 1, 2 * CAP), F32),
        name="gate_totals",
    )(parts)


def pick_kernel(place_ref, ids_ref, pick_ref, gate_ref, back_ref, out_ref):
    masks, _, rank = route_masks(ids_ref, pick_ref, place_ref)
    parts = back_ref.shape[0]
    spread = (
        lax.broadcasted_iota(jnp.int32, (INSTANCES, parts), 0) // 2
        == lax.broadcasted_iota(jnp.int32, (INSTANCES, parts), 1) % (INSTANCES // 2)
    ).astype(F32)
    back = jnp.dot(
        spread,
        back_ref[...].reshape(parts, 2 * CAP),
        precision=lax.Precision.HIGHEST,
        preferred_element_type=F32,
    )
    odd = lax.broadcasted_iota(jnp.int32, (INSTANCES, 1), 0) % 2 == 1
    value = jnp.zeros((INSTANCES, TOK), F32)
    for c in range(CAP):
        column = jnp.where(odd, back[:, CAP + c : CAP + c + 1], back[:, c : c + 1])
        value = jnp.where(rank == c, jnp.broadcast_to(column, (INSTANCES, TOK)), value)
    for k in range(TOP):
        total = jnp.sum(masks[k] * value, axis=0, keepdims=True)
        low = gate_ref[k : k + 1, :].astype(BF16).astype(F32)
        out_ref[k : k + 1, :] = total / low


def pick_gates(placement, ids, pick, gates, back):
    vmem = pl.BlockSpec(memory_space=pltpu.VMEM)
    return pl.pallas_call(
        pick_kernel,
        in_specs=[pl.BlockSpec(memory_space=pltpu.SMEM)] + [vmem] * 4,
        out_specs=vmem,
        out_shape=jax.ShapeDtypeStruct((TOP, TOK), F32),
        name="pick_gates",
    )(placement, ids, pick, gates, back)


LINES = ("y", "c")
EXPERT = ("zh", "x")
GROUPS = ("zl",) + LINES
EVERY = GROUPS + EXPERT


def layer(grad_out, gate_weights, route_ids, replica_pick, placement, hidden_act, down_proj):
    dp, expert = lax.axis_size(GROUPS), lax.axis_size(EXPERT)
    depth = lax.axis_size("zl")
    ff = hidden_act.shape[4]
    local = hidden_act[0].transpose(1, 0, 2, 3).reshape(1, 2, expert * CAP, ff)
    column = [local] + [
        lax.ppermute(local, "zl", [(z, (z + d) % depth) for z in range(depth)])
        for d in range(1, depth)
    ]
    column = jnp.concatenate(column, axis=0)
    pieces = [column]
    for d in range(1, lax.axis_size("y")):
        pieces.append(lax.ppermute(column, "y", [(y, (y + d) % 4) for y in range(4)]))
    pieces = pieces + [lax.ppermute(piece, "c", [(0, 1), (1, 0)]) for piece in pieces]
    place = jnp.stack([lax.axis_index(axis) for axis in GROUPS]).astype(jnp.int32)
    ids, pick, gates = route_ids.T, replica_pick.T, gate_weights.T
    sent = gather_rows(placement, ids, pick, gates, grad_out)
    sent = sent.reshape(dp * expert, 2 * CAP, WIDE)
    rows = lax.all_to_all(sent, EVERY, split_axis=0, concat_axis=0, tiled=True)
    rows = rows.reshape(dp * expert * 2 * CAP, WIDE)
    hot, hot_sent = weight_parts(0, place, rows, pieces)
    half = expert // 2
    other = lax.ppermute(hot_sent, EXPERT, [(e, (e + half) % expert) for e in range(expert)])
    parts = gate_parts(place, rows, pieces, down_proj)
    parts = lax.all_to_all(parts, LINES, split_axis=0, concat_axis=0, tiled=True)
    grad = weight_parts(1, place, rows, pieces)
    own = gate_totals(parts, expert)
    back = lax.all_to_all(own, ("zl",) + EXPERT, split_axis=0, concat_axis=0, tiled=True)
    grad_gate = pick_gates(placement, ids, pick, gates, back).T
    pair = (hot + other.astype(F32)).astype(BF16)
    return lax.dynamic_update_slice(grad, pair[None], (0, 0, 0)), grad_gate


def solution(mesh):
    fine = jax.sharding.Mesh(mesh.devices.reshape(4, 4, 2, 4, 4), EVERY)
    token = P(EVERY, None)
    return jax.shard_map(
        layer,
        mesh=fine,
        in_specs=(
            token,
            token,
            token,
            token,
            P(),
            P(GROUPS, None, EXPERT, None, None),
            P(EXPERT, GROUPS, None),
        ),
        out_specs=(P(EXPERT, GROUPS, None), token),
        check_vma=False,
    )
```

```python
import functools
import jax
import jax.numpy as jnp
from jax import lax
from jax.experimental import pallas as pl
from jax.experimental.pallas import tpu as pltpu
from jax.sharding import PartitionSpec as P


F32 = jnp.float32
BF16 = jnp.bfloat16
INSTANCES = 32
CAP = 4
TOP = 8
TOK = 128
SLOTS = INSTANCES * CAP
PIECE = 224
WIDE = 256
GRANT = 24 * 2**20


def route_masks(ids_ref, pick_ref, place_ref):
    rows = lax.broadcasted_iota(jnp.int32, (INSTANCES, TOK), 0)
    place = jnp.zeros((INSTANCES, TOK), jnp.int32)
    for i in range(INSTANCES):
        place = jnp.where(rows == i, place_ref[i], place)
    single = rows % 2 == 1
    first = rows < INSTANCES // 2
    masks = []
    for k in range(TOP):
        low = jnp.broadcast_to(pick_ref[k : k + 1, :], (INSTANCES, TOK)) == 0
        serves = jnp.logical_or(single, low == first)
        same = jnp.broadcast_to(ids_ref[k : k + 1, :], (INSTANCES, TOK)) == place
        masks.append(jnp.where(jnp.logical_and(same, serves), 1.0, 0.0).astype(F32))
    taken = functools.reduce(jnp.add, masks)
    before = (
        lax.broadcasted_iota(jnp.int32, (TOK, TOK), 0)
        < lax.broadcasted_iota(jnp.int32, (TOK, TOK), 1)
    ).astype(F32)
    rank = jnp.dot(taken.astype(BF16), before.astype(BF16), preferred_element_type=F32)
    return masks, taken, rank


def gather_kernel(place_ref, ids_ref, pick_ref, gate_ref, grad_ref, out_ref, select_ref):
    @pl.when(pl.program_id(0) == 0)
    def _():
        masks, _, rank = route_masks(ids_ref, pick_ref, place_ref)
        gates = jnp.zeros((INSTANCES, TOK), F32)
        for k in range(TOP):
            low = gate_ref[k : k + 1, :].astype(BF16).astype(F32)
            gates = gates + masks[k] * jnp.broadcast_to(low, (INSTANCES, TOK))
        spread = (
            lax.broadcasted_iota(jnp.int32, (SLOTS, INSTANCES), 0) // CAP
            == lax.broadcasted_iota(jnp.int32, (SLOTS, INSTANCES), 1)
        ).astype(F32).astype(BF16)
        slot_rank = jnp.dot(spread, rank.astype(BF16), preferred_element_type=F32)
        slot_gate = jnp.dot(spread, gates.astype(BF16), preferred_element_type=F32)
        own = (lax.broadcasted_iota(jnp.int32, (SLOTS, TOK), 0) % CAP).astype(F32)
        select_ref[...] = jnp.where(slot_rank == own, slot_gate, 0.0).astype(BF16)

    rows = jnp.dot(select_ref[...], grad_ref[...], preferred_element_type=F32)
    blank = jnp.zeros((SLOTS, WIDE - PIECE), F32)
    for j in range(out_ref.shape[0]):
        part = jnp.concatenate([rows[:, j * PIECE : (j + 1) * PIECE], blank], axis=1)
        out_ref[j] = part.astype(BF16)


def gather_rows(placement, ids, pick, gates, grad_out):
    width = grad_out.shape[1]
    per = 8
    steps = width // (per * PIECE)
    whole = pl.BlockSpec((TOP, TOK), lambda s: (0, 0))
    return pl.pallas_call(
        gather_kernel,
        grid=(steps,),
        in_specs=[
            pl.BlockSpec(memory_space=pltpu.SMEM),
            whole,
            whole,
            whole,
            pl.BlockSpec((TOK, per * PIECE), lambda s: (0, s)),
        ],
        out_specs=pl.BlockSpec((per, SLOTS, WIDE), lambda s: (s, 0, 0)),
        out_shape=jax.ShapeDtypeStruct((steps * per, SLOTS, WIDE), BF16),
        scratch_shapes=[pltpu.VMEM((SLOTS, TOK), BF16)],
        cost_estimate=pl.CostEstimate(
            flops=2 * SLOTS * TOK * width, bytes_accessed=4 * TOK * width, transcendentals=0
        ),
        name="gather_rows",
    )(placement, ids, pick, gates, grad_out)


def swap_halves(first, second):
    count, lanes = first.shape
    first, second = first.reshape(count // 8, 8, lanes), second.reshape(count // 8, 8, lanes)
    upper = lax.broadcasted_iota(jnp.int32, first.shape, 1) < CAP
    return (
        jnp.where(upper, first, pltpu.roll(second, 4, 1)).reshape(count, lanes),
        jnp.where(upper, pltpu.roll(first, 4, 1), second).reshape(count, lanes),
    )


def piece_lines(place_ref):
    lines = []
    for other in range(2):
        for d in range(4):
            y = lax.rem(place_ref[1] - d + 4, 4)
            core = place_ref[2] if other == 0 else 1 - place_ref[2]
            lines.append(y * 2 + core)
    return lines


def instance_rows(rows_ref, lines):
    span = rows_ref.shape[0] // len(lines)
    rows = [rows_ref[pl.ds(pl.multiple_of(n * span, span), span), :].astype(F32) for n in lines]
    count = rows_ref.shape[0] // 2
    both = jnp.concatenate(rows, axis=0).reshape(count // 8, 2, 8, WIDE)
    return swap_halves(both[:, 0].reshape(count, WIDE), both[:, 1].reshape(count, WIDE))


def folded_dots(rows, hidden, weight):
    result = lax.dot_general(hidden, weight, (((1,), (1,)), ((), ())), preferred_element_type=F32)
    product = result * rows[:, :PIECE]
    blank = jnp.zeros((rows.shape[0], WIDE - PIECE), F32)
    return product[:, :128] + jnp.concatenate([product[:, 128:PIECE], blank], axis=1)


def add_grad(acc_ref, rows, hidden):
    grad = lax.dot_general(
        rows[:, :PIECE].astype(BF16), hidden, (((0,), (0,)), ((), ())), preferred_element_type=F32
    )

    @pl.when(pl.program_id(0) == 0)
    def _():
        acc_ref[...] = grad

    @pl.when(pl.program_id(0) != 0)
    def _():
        acc_ref[...] += grad


def gate_kernel(place_ref, rows_ref, weight_ref, *refs):
    pieces, gate_ref = refs[:-1], refs[-1]
    lines = piece_lines(place_ref)
    split = instance_rows(rows_ref, lines)
    count = rows_ref.shape[0] // 2
    hidden = [jnp.concatenate([piece[i] for piece in pieces], axis=0) for i in range(2)]
    even, odd = swap_halves(*(folded_dots(split[i], hidden[i], weight_ref[i]) for i in range(2)))
    both = jnp.concatenate(
        [even.reshape(count // 8, 1, 8, 128), odd.reshape(count // 8, 1, 8, 128)], axis=1
    )
    both = both.reshape(count * 2 // 128, 128, 128)
    for g, line in enumerate(lines):
        gate_ref[line, 0] = jnp.sum(both[g].T, axis=0, keepdims=True)


def hot_kernel(place_ref, rows_ref, *refs):
    pieces, (send_ref, acc_ref) = refs[:-2], refs[-2:]
    hidden = jnp.concatenate([piece[...] for piece in pieces], axis=0)
    add_grad(acc_ref, instance_rows(rows_ref, piece_lines(place_ref))[0], hidden)

    @pl.when(pl.program_id(0) == pl.num_programs(0) - 1)
    def _():
        send_ref[...] = acc_ref[...].astype(BF16)


def cold_kernel(place_ref, rows_ref, *refs):
    pieces, (out_ref, acc_ref) = refs[:-2], refs[-2:]
    hidden = jnp.concatenate([piece[...] for piece in pieces], axis=0)
    add_grad(acc_ref, instance_rows(rows_ref, piece_lines(place_ref))[1], hidden)

    @pl.when(pl.program_id(0) == pl.num_programs(0) - 1)
    def _():
        out_ref[0] = acc_ref[...].astype(BF16)


def piece_index(s, m, instance):
    return (lax.rem(m[0] - s + 4, 4), instance, 0, 0)


def gate_parts(place, rows, pieces, weight):
    steps, _, span, ff = pieces[0].shape
    lines = len(pieces)
    return pl.pallas_call(
        gate_kernel,
        grid_spec=pltpu.PrefetchScalarGridSpec(
            num_scalar_prefetch=1,
            grid=(steps,),
            in_specs=[
                pl.BlockSpec((lines * span * 2, WIDE), lambda s, m: (s, 0)),
                pl.BlockSpec((2, PIECE, ff), lambda s, m: (0, 0, 0)),
            ]
            + [pl.BlockSpec((None, 2, span, ff), lambda s, m: piece_index(s, m, 0))] * lines,
            out_specs=pl.BlockSpec((lines, 1, 1, 2 * span), lambda s, m: (0, s, 0, 0)),
        ),
        out_shape=jax.ShapeDtypeStruct((lines, steps, 1, 2 * span), F32),
        cost_estimate=pl.CostEstimate(
            flops=4 * lines * steps * span * PIECE * ff,
            bytes_accessed=4 * lines * steps * span * ff + 2 * rows.size + 2 * weight.size,
            transcendentals=0,
        ),
        compiler_params=pltpu.CompilerParams(vmem_limit_bytes=GRANT),
        name="gate_parts",
    )(place, rows, weight, *pieces)


def weight_parts(which, place, rows, pieces):
    steps, _, span, ff = pieces[0].shape
    lines = len(pieces)
    hot = which == 0
    whole = pl.BlockSpec((PIECE, ff), lambda s, m: (0, 0))
    half = pl.BlockSpec((1, PIECE, ff), lambda s, m: (1, 0, 0))
    return pl.pallas_call(
        hot_kernel if hot else cold_kernel,
        grid_spec=pltpu.PrefetchScalarGridSpec(
            num_scalar_prefetch=1,
            grid=(steps,),
            in_specs=[pl.BlockSpec((lines * span * 2, WIDE), lambda s, m: (s, 0))]
            + [pl.BlockSpec((None, None, span, ff), lambda s, m: piece_index(s, m, which))] * lines,
            out_specs=whole if hot else half,
            scratch_shapes=[pltpu.VMEM((PIECE, ff), F32)],
        ),
        out_shape=jax.ShapeDtypeStruct((PIECE, ff) if hot else (2, PIECE, ff), BF16),
        cost_estimate=pl.CostEstimate(
            flops=2 * lines * steps * span * PIECE * ff,
            bytes_accessed=2 * lines * steps * span * ff + 2 * rows.size,
            transcendentals=0,
        ),
        compiler_params=pltpu.CompilerParams(vmem_limit_bytes=GRANT),
        name="hot_parts" if hot else "cold_parts",
    )(place, rows, *pieces)


def total_kernel(parts_ref, out_ref):
    steps = parts_ref.shape[1]
    experts = out_ref.shape[0] // steps
    total = jnp.sum(parts_ref[...], axis=0)
    for z in range(steps):
        for e in range(experts):
            out_ref[z * experts + e] = total[z, :, e * 2 * CAP : (e + 1) * 2 * CAP]


def gate_totals(parts, expert):
    vmem = pl.BlockSpec(memory_space=pltpu.VMEM)
    return pl.pallas_call(
        total_kernel,
        in_specs=[vmem],
        out_specs=vmem,
        out_shape=jax.ShapeDtypeStruct((parts.shape[1] * expert, 1, 2 * CAP), F32),
        compiler_params=pltpu.CompilerParams(vmem_limit_bytes=GRANT),
        name="gate_totals",
    )(parts)


def pick_kernel(place_ref, ids_ref, pick_ref, gate_ref, back_ref, out_ref):
    masks, _, rank = route_masks(ids_ref, pick_ref, place_ref)
    parts = back_ref.shape[0]
    spread = (
        lax.broadcasted_iota(jnp.int32, (INSTANCES, parts), 0) // 2
        == lax.broadcasted_iota(jnp.int32, (INSTANCES, parts), 1) % (INSTANCES // 2)
    ).astype(F32)
    back = jnp.dot(
        spread,
        back_ref[...].reshape(parts, 2 * CAP),
        precision=lax.Precision.HIGHEST,
        preferred_element_type=F32,
    )
    odd = lax.broadcasted_iota(jnp.int32, (INSTANCES, 1), 0) % 2 == 1
    value = jnp.zeros((INSTANCES, TOK), F32)
    for c in range(CAP):
        column = jnp.where(odd, back[:, CAP + c : CAP + c + 1], back[:, c : c + 1])
        value = jnp.where(rank == c, jnp.broadcast_to(column, (INSTANCES, TOK)), value)
    for k in range(TOP):
        total = jnp.sum(masks[k] * value, axis=0, keepdims=True)
        low = gate_ref[k : k + 1, :].astype(BF16).astype(F32)
        out_ref[k : k + 1, :] = total / low


def pick_gates(placement, ids, pick, gates, back):
    vmem = pl.BlockSpec(memory_space=pltpu.VMEM)
    return pl.pallas_call(
        pick_kernel,
        in_specs=[pl.BlockSpec(memory_space=pltpu.SMEM)] + [vmem] * 4,
        out_specs=vmem,
        out_shape=jax.ShapeDtypeStruct((TOP, TOK), F32),
        compiler_params=pltpu.CompilerParams(vmem_limit_bytes=GRANT),
        name="pick_gates",
    )(placement, ids, pick, gates, back)


LINES = ("y", "c")
EXPERT = ("zh", "x")
GROUPS = ("zl",) + LINES
EVERY = GROUPS + EXPERT


def layer(grad_out, gate_weights, route_ids, replica_pick, placement, hidden_act, down_proj):
    dp, expert = lax.axis_size(GROUPS), lax.axis_size(EXPERT)
    depth = lax.axis_size("zl")
    ff = hidden_act.shape[4]
    local = hidden_act[0].transpose(1, 0, 2, 3).reshape(1, 2, expert * CAP, ff)
    column = [local] + [
        lax.ppermute(local, "zl", [(z, (z + d) % depth) for z in range(depth)])
        for d in range(1, depth)
    ]
    column = jnp.concatenate(column, axis=0)
    pieces = [column]
    for d in range(1, lax.axis_size("y")):
        pieces.append(lax.ppermute(column, "y", [(y, (y + d) % 4) for y in range(4)]))
    pieces = pieces + [lax.ppermute(piece, "c", [(0, 1), (1, 0)]) for piece in pieces]
    place = jnp.stack([lax.axis_index(axis) for axis in GROUPS]).astype(jnp.int32)
    ids, pick, gates = route_ids.T, replica_pick.T, gate_weights.T
    sent = gather_rows(placement, ids, pick, gates, grad_out)
    sent = sent.reshape(dp * expert, 2 * CAP, WIDE)
    rows = lax.all_to_all(sent, EVERY, split_axis=0, concat_axis=0, tiled=True)
    rows = rows.reshape(dp * expert * 2 * CAP, WIDE)
    hot = weight_parts(0, place, rows, pieces)
    half = expert // 2
    other = lax.ppermute(hot, EXPERT, [(e, (e + half) % expert) for e in range(expert)])
    parts = gate_parts(place, rows, pieces, down_proj)
    parts = lax.all_to_all(parts, LINES, split_axis=0, concat_axis=0, tiled=True)
    grad = weight_parts(1, place, rows, pieces)
    own = gate_totals(parts, expert)
    back = lax.all_to_all(own, ("zl",) + EXPERT, split_axis=0, concat_axis=0, tiled=True)
    grad_gate = pick_gates(placement, ids, pick, gates, back).T
    pair = (hot.astype(F32) + other.astype(F32)).astype(BF16)
    return lax.dynamic_update_slice(grad, pair[None], (0, 0, 0)), grad_gate


def solution(mesh):
    fine = jax.sharding.Mesh(mesh.devices.reshape(4, 4, 2, 4, 4), EVERY)
    token = P(EVERY, None)
    return jax.shard_map(
        layer,
        mesh=fine,
        in_specs=(
            token,
            token,
            token,
            token,
            P(),
            P(GROUPS, None, EXPERT, None, None),
            P(EXPERT, GROUPS, None),
        ),
        out_specs=(P(EXPERT, GROUPS, None), token),
        check_vma=False,
    )
```
